768 devices in a mesh: gx: 64 (over y, x, core), gz: 12 (over z).
Axes of the slice: x: 4, y: 8, z: 12, core: 2. Of those that a mesh axis runs over, the one named last changes fastest.
Arguments:
- velocity: bfloat16 [2, 128, 2, 1536, 1536], P(None, None, None, 'gx', 'gz'), may hold values from -8 to 8
- snapshot_rank: int32 [128], replicated, may hold values from 0 to 127, each once
- anchor_index: int32 [64], replicated, may hold values from 0 to 4718591
- start_basis: float32 [128, 64], replicated, may hold values from -6 to 6
Outputs:
- modes: bfloat16 [64, 2, 1536, 1536], P(None, None, 'gx', 'gz')
- basis: float32 [128, 64], replicated
The draws below stay inside these ranges and needn't reach their ends.
All inputs are finite; a program needn't handle non-finite values.
Results may differ from the reference program's by a relative error of at most 0.0073.
Values may be sent and summed in bfloat16 or wider, within the bound.
No kernel may reach another device: no remote copies, remote signals or barrier semaphores. Data moves between devices by JAX's collectives and lax.ppermute only.
A program may use at most 32 MiB of HBM per device.

```python
import math
import jax
import jax.numpy as jnp
from jax import lax

M = 128
K = 64
P_SIZE = 2
ITERS = 3
NX = 1536
NZ = 1536
NCELLS = 4718592


def draw_velocity(key, part):
    field_count = 32
    mixing_key = jax.random.fold_in(key, 101)
    stream_key = jax.random.fold_in(key, 202)
    span_key = jax.random.fold_in(key, 303)
    spread_key = jax.random.fold_in(key, 404)
    noise_key = jax.random.fold_in(key, 505)
    fields_key = jax.random.fold_in(key, 707)
    mixing = jax.random.normal(mixing_key, (M, field_count), jnp.float32) * (0.5 / math.sqrt(field_count))
    env_low = 0.5
    env_high = 2.0
    stream_envelope = jnp.exp(jax.random.uniform(stream_key, (field_count, NX), jnp.float32, math.log(env_low), math.log(env_high)))
    span_envelope = jnp.exp(jax.random.uniform(span_key, (field_count, NZ), jnp.float32, math.log(env_low), math.log(env_high)))
    spread = jnp.exp(jax.random.uniform(spread_key, (M,), jnp.float32, 0.0, math.log(1.6)))
    noise = jax.random.truncated_normal(noise_key, -6.0, 6.0, (2, M, P_SIZE, NX, NZ), jnp.float32)
    accumulated = noise * spread[None, :, None, None, None]

    def add_field(index, carried):
        field_key = jax.random.fold_in(fields_key, index)
        field = jax.random.truncated_normal(field_key, -6.0, 6.0, (2, P_SIZE, NX, NZ), jnp.float32)
        field = field * stream_envelope[index][None, None, :, None] * span_envelope[index][None, None, None, :]
        return carried + mixing[:, index][None, :, None, None, None] * field[:, None]
    accumulated = lax.fori_loop(0, field_count, add_field, accumulated)
    return jnp.clip(accumulated, -8.0, 8.0).astype(jnp.bfloat16)


def with_ends(drawn, rng, least, largest):
    index_at = [jax.random.randint(jax.random.fold_in(rng, axis), (), 0, length) for axis, length in enumerate(drawn.shape)]
    longest = drawn.shape.index(max(drawn.shape))
    next_to = index_at[:longest] + [(index_at[longest] + 1) % drawn.shape[longest]] + index_at[longest + 1:]
    return drawn.at[tuple(index_at)].set(least).at[tuple(next_to)].set(largest)


def centred(own_key, shape, width, limit, held_as=jnp.bfloat16):
    values = width * jax.random.normal(own_key, shape, jnp.float32)
    return jnp.clip(values, min=-limit, max=limit).astype(held_as)


def setup_inputs(seed: int = 0) -> dict:
    streams_of = jax.random.split(jax.random.key(seed), 5)
    return {
        "velocity": draw_velocity(jax.random.fold_in(streams_of[4], 71), 0),
        "snapshot_rank": jax.random.permutation(streams_of[1], M).astype(jnp.int32),
        "anchor_index": with_ends(jax.random.randint(streams_of[2], (K,), 0, NCELLS), jax.random.fold_in(streams_of[2], 1), 0, NCELLS - 1).astype(jnp.int32),
        "start_basis": centred(streams_of[3], (M, K), 1.0, 6.0, jnp.float32),
    }


def vorticity(field):
    upart = field[0].astype(jnp.float32)
    wpart = field[1].astype(jnp.float32)
    weights = (45.0 / 60.0, -9.0 / 60.0, 1.0 / 60.0)
    total = jnp.zeros(upart.shape, jnp.float32)
    for shift_by in range(1, 4):
        weight_now = weights[shift_by - 1]
        total = total + weight_now * (jnp.roll(wpart, -shift_by, axis=1) - jnp.roll(wpart, shift_by, axis=1))
        total = total - weight_now * (jnp.roll(upart, -shift_by, axis=2) - jnp.roll(upart, shift_by, axis=2))
    return total.astype(jnp.bfloat16)

def orthonormal(block):
    inner = jnp.dot(block.T, block, precision=lax.Precision.HIGHEST)
    lower = jnp.linalg.cholesky(inner)
    return jax.scipy.linalg.solve_triangular(lower, block.T, lower=True).T

def reference(velocity, snapshot_rank, anchor_index, start_basis):
    vort = lax.map(vorticity, jnp.moveaxis(velocity, 1, 0))
    flat = vort.reshape(M, NCELLS)
    gram = lax.dot_general(flat.astype(jnp.float32), flat.astype(jnp.float32), (((1,), (1,)), ((), ())), preferred_element_type=jnp.float32)
    gram = gram / float(NCELLS)
    scale = jnp.where(snapshot_rank < K, 1.0, 0.25).astype(jnp.float32)
    weighted = scale[:, None] * gram * scale[None, :]
    basis_now = start_basis
    for step in range(ITERS):
        basis_now = orthonormal(jnp.dot(weighted, basis_now, precision=lax.Precision.HIGHEST))
    coef = (scale[:, None] * basis_now).astype(jnp.bfloat16)
    picked = flat[:, anchor_index].astype(jnp.float32)
    anchor = jnp.sum(picked * coef.astype(jnp.float32), axis=0)
    orient = anchor / jnp.maximum(jnp.abs(anchor), 1.0)
    raw = lax.dot_general(coef.astype(jnp.float32), flat.astype(jnp.float32), (((0,), (0,)), ((), ())), preferred_element_type=jnp.float32)
    modes = (raw * orient[:, None]).astype(jnp.bfloat16).reshape(K, P_SIZE, NX, NZ)
    return (modes, basis_now * orient[None, :])
```

```python
import jax
import jax.numpy as jnp
from jax import lax
from jax.sharding import PartitionSpec as P

ITERS = 3


def extended(cells, sides, width):
    for axis, dim in sides:
        count = lax.axis_size(axis)
        head = lax.slice_in_dim(cells, 0, width, axis=dim)
        tail = lax.slice_in_dim(cells, cells.shape[dim] - width, cells.shape[dim], axis=dim)
        cells = jnp.concatenate(
            [
                lax.ppermute(tail, axis, [(i, (i + 1) % count) for i in range(count)]),
                cells,
                lax.ppermute(head, axis, [((i + 1) % count, i) for i in range(count)]),
            ],
            axis=dim,
        )
    return cells


def orthonormal(block):
    inner = jnp.dot(block.T, block, precision=lax.Precision.HIGHEST)
    lower = jnp.linalg.cholesky(inner)
    return jax.scipy.linalg.solve_triangular(lower, block.T, lower=True).T


def local_position(anchor_index, planes, cols_x, cols_z, total_x, total_z):
    plane_of = anchor_index // (total_x * total_z)
    remain = anchor_index % (total_x * total_z)
    local_x = remain // total_z - lax.axis_index("gx") * cols_x
    local_z = remain % total_z - lax.axis_index("gz") * cols_z
    owned = (local_x >= 0) & (local_x < cols_x) & (local_z >= 0) & (local_z < cols_z)
    return jnp.where(owned, (plane_of * cols_x + local_x) * cols_z + local_z, -1)


def exchanged(rows, axis):
    return lax.all_to_all(rows, axis, 0, 0, tiled=True)


def total_of(local, snaps, kept):
    count_x = lax.axis_size("gx")
    count_z = lax.axis_size("gz")
    width = local.shape[1]
    blocks = local.shape[0] // count_x
    rows = jnp.concatenate([local[b * count_x : (b + 1) * count_x] for b in range(blocks)], axis=1)
    mine = jnp.sum(exchanged(rows, "gx"), axis=0)
    mine = jnp.sum(exchanged(jnp.broadcast_to(mine, (count_z,) + mine.shape), "gz"), axis=0)
    rows = exchanged(jnp.broadcast_to(mine, (count_x,) + mine.shape), "gx")
    whole = jnp.concatenate([rows[:, b * width : (b + 1) * width] for b in range(blocks)], axis=0)
    return whole[:snaps], whole[snaps:]


def body(velocity, snapshot_rank, anchor_index, start_basis):
    snaps = velocity.shape[1]
    planes = velocity.shape[2]
    cols_x = velocity.shape[3]
    cols_z = velocity.shape[4]
    kept = start_basis.shape[1]
    wide_w = extended(velocity[1], (("gx", 2),), 3)
    wide_u = extended(velocity[0], (("gz", 3),), 3)
    weights = (45.0 / 60.0, -9.0 / 60.0, 1.0 / 60.0)
    total = jnp.zeros((snaps, planes, cols_x, cols_z), jnp.float32)
    for shift_by in range(1, 4):
        weight_now = weights[shift_by - 1]
        ahead_w = wide_w[:, :, 3 + shift_by : 3 + shift_by + cols_x, :].astype(jnp.float32)
        behind_w = wide_w[:, :, 3 - shift_by : 3 - shift_by + cols_x, :].astype(jnp.float32)
        ahead_u = wide_u[:, :, :, 3 + shift_by : 3 + shift_by + cols_z].astype(jnp.float32)
        behind_u = wide_u[:, :, :, 3 - shift_by : 3 - shift_by + cols_z].astype(jnp.float32)
        total = total + weight_now * (ahead_w - behind_w) - weight_now * (ahead_u - behind_u)
    flat = total.astype(jnp.bfloat16).reshape(snaps, planes * cols_x * cols_z)
    count_x = lax.axis_size("gx")
    count_z = lax.axis_size("gz")
    total_x = cols_x * count_x
    total_z = cols_z * count_z
    position = local_position(anchor_index, planes, cols_x, cols_z, total_x, total_z)
    cell_of = lax.broadcasted_iota(jnp.int32, (kept, planes * cols_x * cols_z), 1)
    chosen = (cell_of == position[:, None]).astype(jnp.bfloat16)
    local = lax.dot_general(
        jnp.concatenate([flat, chosen], axis=0),
        flat,
        (((1,), (1,)), ((), ())),
        preferred_element_type=jnp.float32,
    )
    gram, picked = total_of(local, snaps, kept)
    gram = gram / float(planes * total_x * total_z)
    scale = jnp.where(snapshot_rank < kept, 1.0, 0.25).astype(jnp.float32)
    weighted = scale[:, None] * gram * scale[None, :]
    basis_now = start_basis
    for step in range(ITERS):
        basis_now = orthonormal(jnp.dot(weighted, basis_now, precision=lax.Precision.HIGHEST))
    coef = (scale[:, None] * basis_now).astype(jnp.bfloat16)
    raw = lax.dot_general(coef, flat, (((0,), (0,)), ((), ())), preferred_element_type=jnp.float32)
    anchor = jnp.sum(picked * coef.T.astype(jnp.float32), axis=1)
    orient = anchor / jnp.maximum(jnp.abs(anchor), 1.0)
    modes = (raw * orient[:, None]).astype(jnp.bfloat16).reshape(kept, planes, cols_x, cols_z)
    return (modes, basis_now * orient[None, :])


def solution(mesh):
    return jax.shard_map(
        body,
        mesh=mesh,
        in_specs=(P(None, None, None, "gx", "gz"), P(), P(), P()),
        out_specs=(P(None, None, "gx", "gz"), P()),
        check_vma=False,
    )
```

```python
from functools import partial

import jax
import jax.numpy as jnp
import numpy as np
from jax import lax
from jax.experimental import pallas as pl
from jax.experimental.pallas import tpu as pltpu
from jax.sharding import PartitionSpec as P

ITERS = 3
REACH = 3
TAPS = (45.0, -9.0, 1.0)
TAP_SUM = 60.0
GROUP = 8
HIGHEST = lax.Precision.HIGHEST
NT = (((1,), (1,)), ((), ()))
TN = (((0,), (0,)), ((), ()))


def tap(offset):
    size = abs(offset)
    if size < 1 or size > REACH:
        return 0.0
    return TAPS[size - 1] if offset > 0 else -TAPS[size - 1]


def band(points, first, count):
    return np.array([[tap(first + j - i) for j in range(count)] for i in range(points)], np.float32)


def tables(planes, cols_x, cols_z):
    lines = planes * cols_x
    eye = np.eye(GROUP, dtype=np.float32)
    order = np.einsum("ab,mn->ambn", np.eye(lines, dtype=np.float32), eye)
    order = order.transpose(0, 1, 3, 2).reshape(lines * GROUP, GROUP * lines)
    along_x = np.kron(np.eye(planes, dtype=np.float32), band(cols_x, 0, cols_x))
    along_x = np.einsum("ab,mn->ambn", along_x, eye).transpose(0, 1, 3, 2)
    along_x = along_x.reshape(lines * GROUP, GROUP * lines)
    along_z = -band(cols_z, 0, cols_z).T
    edge_z = np.zeros((2 * GROUP, cols_z), np.float32)
    edge_z[:REACH] = -band(cols_z, cols_z, REACH).T
    edge_z[GROUP : GROUP + REACH] = -band(cols_z, -REACH, REACH).T
    ends_z = np.zeros((2 * GROUP, cols_z), np.float32)
    ends_x = np.zeros((2, REACH, planes, GROUP, GROUP, planes, cols_x), np.float32)
    for h in range(REACH):
        ends_z[h, h] = 1.0
        ends_z[GROUP + h, cols_z - REACH + h] = 1.0
        for p in range(planes):
            for m in range(GROUP):
                ends_x[0, h, p, m, m, p, h] = 1.0
                ends_x[1, h, p, m, m, p, cols_x - REACH + h] = 1.0
    ends_x = ends_x.reshape(2 * REACH * planes * GROUP, GROUP * lines)
    cast = lambda table: jnp.asarray(table, jnp.bfloat16)
    return {
        "order": cast(order),
        "order_t": cast(order.T),
        "along_x": cast(along_x),
        "along_z": cast(along_z),
        "edge_z": cast(edge_z),
        "ends_z": cast(ends_z),
        "ends_x": cast(ends_x),
    }


def matmul(left, right, dims=None):
    dims = dims or (((1,), (0,)), ((), ()))
    return lax.dot_general(left, right, dims, preferred_element_type=jnp.float32)


def flat_group(ref, field, group):
    block = ref[field, pl.ds(group * GROUP, GROUP)]
    return block.reshape(-1, block.shape[-1])


def ends_kernel(velocity, ends_x, ends_z, order_t, head_w, tail_w, head_u, tail_u):
    planes = velocity.shape[2]
    for q in range(velocity.shape[1] // GROUP):
        rows = matmul(ends_x[...], flat_group(velocity, 1, q)).astype(jnp.bfloat16)
        here = pl.ds(q * GROUP, GROUP)
        for h in range(REACH):
            for p in range(planes):
                at = (h * planes + p) * GROUP
                head_w[h, p, here, :] = rows[at : at + GROUP]
                at = at + REACH * planes * GROUP
                tail_w[h, p, here, :] = rows[at : at + GROUP]
        cols = matmul(ends_z[...], flat_group(velocity, 0, q), NT).astype(jnp.bfloat16)
        cols = matmul(cols, order_t[...]).astype(jnp.bfloat16)
        head_u[here, :] = cols[:GROUP]
        tail_u[here, :] = cols[GROUP:]


def inner_kernel(velocity, along_x, along_z, order, out):
    lines = out.shape[0]
    cols_z = out.shape[2]
    for q in range(0, velocity.shape[1] // GROUP, 2):
        w_two = jnp.concatenate([flat_group(velocity, 1, q), flat_group(velocity, 1, q + 1)], axis=1)
        u_two = jnp.concatenate([flat_group(velocity, 0, q), flat_group(velocity, 0, q + 1)], axis=1)
        part = matmul(along_x[...], w_two)
        moved = matmul(order[...], u_two).astype(jnp.bfloat16)
        for half in range(2):
            lanes = slice(half * cols_z, (half + 1) * cols_z)
            value = part[:, lanes] + matmul(moved[:, lanes], along_z[...])
            out[:, pl.ds((q + half) * GROUP, GROUP), :] = value.reshape(lines, GROUP, cols_z)


def gram_kernel(planes, cols_x, inner, left_w, right_w, left_u, right_u, edge_z, place, vort, rows_out, work):
    lines, snaps, cols_z = inner.shape
    kept = place.shape[0]
    for q in range(snaps // GROUP):
        here = pl.ds(q * GROUP, GROUP)
        cols = jnp.concatenate([right_u[here, :], left_u[here, :]], axis=0)
        value = matmul(cols, edge_z[...], TN).reshape(lines, GROUP, cols_z)
        work[:, here, :] = inner[:, here, :] + value
    gram = jnp.zeros((snaps + kept, snaps), jnp.float32)
    lane = lax.broadcasted_iota(jnp.int32, (kept, 2 * cols_z), 1)
    for pair in range(lines // 2):
        sides = []
        for line in (2 * pair, 2 * pair + 1):
            p, x = line // cols_x, line % cols_x
            value = work[line]
            for h in range(REACH):
                if tap(cols_x + h - x):
                    value = value + tap(cols_x + h - x) * right_w[h, p].astype(jnp.float32)
                if tap(h - REACH - x):
                    value = value + tap(h - REACH - x) * left_w[h, p].astype(jnp.float32)
            value = (value * (1.0 / TAP_SUM)).astype(jnp.bfloat16)
            vort[line] = value
            sides.append(value)
        both = jnp.concatenate(sides, axis=1)
        chosen = jnp.where(lane == place[...] - 2 * pair * cols_z, 1.0, 0.0).astype(jnp.bfloat16)
        gram = gram + matmul(jnp.concatenate([both, chosen], axis=0), both, NT)
    for part in range((snaps + kept) // kept):
        rows_out[:, part * snaps : (part + 1) * snaps] = gram[part * kept : (part + 1) * kept]


def inverse_root(value):
    root = lax.rsqrt(value)
    return root * (1.5 - 0.5 * value * root * root)


def orthonormal_rows(block, inner):
    kept, snaps = block.shape
    tile = (GROUP, snaps)
    count = kept // GROUP
    row_at = lax.broadcasted_iota(jnp.int32, tile, 0)
    inner_rows = [inner[GROUP * i : GROUP * (i + 1)] for i in range(count)]
    block_rows = [block[GROUP * i : GROUP * (i + 1)] for i in range(count)]
    for b in range(count):
        first = GROUP * b
        cols = [
            [jnp.broadcast_to(inner_rows[r][:, first + t : first + t + 1], tile) for r in range(b, count)]
            for t in range(GROUP)
        ]
        for t in range(GROUP):
            root = inverse_root(jnp.broadcast_to(cols[t][0][t : t + 1], tile))
            factor = [col * root for col in cols[t]]
            below = jnp.where(row_at > t, factor[0], 0.0)
            inner_row = jnp.broadcast_to(inner_rows[b][t : t + 1], (GROUP, kept)) * root[:, :kept]
            block_row = jnp.broadcast_to(block_rows[b][t : t + 1], tile) * root
            for later in range(t + 1, GROUP):
                share = jnp.broadcast_to(factor[0][later : later + 1], tile)
                cols[later] = [col - part * share for col, part in zip(cols[later], factor)]
            inner_rows[b] = inner_rows[b] - below[:, :kept] * inner_row
            block_rows[b] = jnp.where(row_at == t, block_row, block_rows[b] - below * block_row)
            for r in range(b + 1, count):
                inner_rows[r] = inner_rows[r] - factor[r - b][:, :kept] * inner_row
                block_rows[r] = block_rows[r] - factor[r - b] * block_row
    return jnp.concatenate(block_rows, axis=0)


def modes_kernel(cells, rows, rank, start, vort, modes, basis, work):
    kept, snaps = start.shape
    lines = vort.shape[0]
    gram = jnp.concatenate(
        [rows[:, b * snaps : (b + 1) * snaps] for b in range(snaps // kept)], axis=0
    ) * (1.0 / cells)
    picked = rows[:, snaps // kept * snaps :]
    scale = jnp.where(rank[...] < kept, 1.0, 0.25).astype(jnp.float32)
    now = start[...]
    for step in range(ITERS):
        block = lax.dot_general(now * scale, gram, NT, precision=HIGHEST, preferred_element_type=jnp.float32)
        block = block * scale
        inner = lax.dot_general(block, block, NT, precision=HIGHEST, preferred_element_type=jnp.float32)
        now = orthonormal_rows(block, inner)
    coef = (now * scale).astype(jnp.bfloat16)
    anchor = jnp.sum(picked * coef.astype(jnp.float32), axis=1, keepdims=True)
    orient = anchor / jnp.maximum(jnp.abs(anchor), 1.0)
    basis[...] = now * orient
    for line in range(lines):
        work[pl.ds(line, kept, stride=lines), :] = matmul(coef, vort[line]) * orient
    modes[...] = work[...].astype(jnp.bfloat16).reshape(modes.shape)


def local_place(anchor_index, planes, cols_x, cols_z, total_x, total_z):
    plane_of = anchor_index // (total_x * total_z)
    remain = anchor_index % (total_x * total_z)
    local_x = remain // total_z - lax.axis_index("gx") * cols_x
    local_z = remain % total_z - lax.axis_index("gz") * cols_z
    owned = (local_x >= 0) & (local_x < cols_x) & (local_z >= 0) & (local_z < cols_z)
    return jnp.where(owned, (plane_of * cols_x + local_x) * cols_z + local_z, -1)


def shifted(value, axis, step):
    count = lax.axis_size(axis)
    return lax.ppermute(value, axis, [(i, (i + step) % count) for i in range(count)])


def exchanged(rows, axis):
    return lax.all_to_all(rows, axis, 0, 0, tiled=True)


def summed(rows, axis):
    count = lax.axis_size(axis)
    return jnp.sum(rows.reshape((count, rows.shape[0] // count) + rows.shape[1:]), axis=0)


def copies(rows, axis):
    return jnp.tile(rows, (lax.axis_size(axis), 1))


def body(velocity, snapshot_rank, anchor_index, start_basis):
    _, snaps, planes, cols_x, cols_z = velocity.shape
    kept = start_basis.shape[1]
    lines = planes * cols_x
    total_x = cols_x * lax.axis_size("gx")
    total_z = cols_z * lax.axis_size("gz")
    table = tables(planes, cols_x, cols_z)
    steps = 4
    share = snaps // steps
    whole = lambda array: pl.BlockSpec(array.shape, lambda i: (0,) * array.ndim)
    velocity_spec = pl.BlockSpec((2, share, planes, cols_x, cols_z), lambda i: (0, i, 0, 0, 0))
    shape = jax.ShapeDtypeStruct
    side_w = pl.BlockSpec((REACH, planes, share, cols_z), lambda i: (0, 0, i, 0))
    side_u = pl.BlockSpec((share, lines * GROUP), lambda i: (i, 0))
    given = [table["ends_x"], table["ends_z"], table["order_t"]]
    head_w, tail_w, head_u, tail_u = pl.pallas_call(
        ends_kernel,
        grid=(steps,),
        in_specs=[velocity_spec] + [whole(t) for t in given],
        out_specs=[side_w, side_w, side_u, side_u],
        out_shape=[shape((REACH, planes, snaps, cols_z), jnp.bfloat16)] * 2
        + [shape((snaps, lines * GROUP), jnp.bfloat16)] * 2,
        name="ends",
    )(velocity, *given)
    left_w = shifted(tail_w, "gx", 1)
    right_w = shifted(head_w, "gx", -1)
    left_u = shifted(tail_u, "gz", 1)
    right_u = shifted(head_u, "gz", -1)
    given = [table["along_x"], table["along_z"], table["order"]]
    inner = pl.pallas_call(
        inner_kernel,
        grid=(steps,),
        in_specs=[velocity_spec] + [whole(t) for t in given],
        out_specs=pl.BlockSpec((lines, share, cols_z), lambda i: (0, i, 0)),
        out_shape=shape((lines, snaps, cols_z), jnp.float32),
        name="inner",
    )(velocity, *given)
    place = local_place(anchor_index, planes, cols_x, cols_z, total_x, total_z)
    vort, rows = pl.pallas_call(
        partial(gram_kernel, planes, cols_x),
        out_shape=[
            shape((lines, snaps, cols_z), jnp.bfloat16),
            shape((kept, (snaps // kept + 1) * snaps), jnp.float32),
        ],
        scratch_shapes=[pltpu.VMEM((lines, snaps, cols_z), jnp.float32)],
        name="gram",
    )(inner, left_w, right_w, left_u, right_u, table["edge_z"], place[:, None])
    mine = summed(exchanged(rows, "gx"), "gx")
    mine = summed(exchanged(copies(mine, "gz"), "gz"), "gz")
    rows = exchanged(copies(mine, "gx"), "gx")
    modes, basis = pl.pallas_call(
        partial(modes_kernel, float(planes * total_x * total_z)),
        out_shape=[
            shape((kept, planes, cols_x, cols_z), jnp.bfloat16),
            shape((kept, snaps), jnp.float32),
        ],
        scratch_shapes=[pltpu.VMEM((kept * lines, cols_z), jnp.float32)],
        name="modes",
    )(rows, snapshot_rank[None, :], start_basis.T, vort)
    return modes, basis.T


def solution(mesh):
    return jax.shard_map(
        body,
        mesh=mesh,
        in_specs=(P(None, None, None, "gx", "gz"), P(), P(), P()),
        out_specs=(P(None, None, "gx", "gz"), P()),
        check_vma=False,
    )
```

```python
from functools import partial

import jax
import jax.numpy as jnp
from jax import lax
from jax.experimental import pallas as pl
from jax.experimental.pallas import tpu as pltpu
from jax.sharding import PartitionSpec as P

ITERS = 3
REACH = 3
TAPS = (45.0, -9.0, 1.0)
TAP_SUM = 60.0
GROUP = 8
FEW = 4
KERNEL_VMEM = 16 << 20
HIGHEST = lax.Precision.HIGHEST
NT = (((1,), (1,)), ((), ()))
TN = (((0,), (0,)), ((), ()))


def tap(offset):
    size = abs(offset)
    if size < 1 or size > REACH:
        return 0.0
    return TAPS[size - 1] if offset > 0 else -TAPS[size - 1]


def taps_at(offset):
    value = jnp.zeros(offset.shape, jnp.float32)
    for size in range(1, REACH + 1):
        value = jnp.where(offset == size, TAPS[size - 1], value)
        value = jnp.where(offset == -size, -TAPS[size - 1], value)
    return value


def index(shape, axis):
    return lax.broadcasted_iota(jnp.int32, shape, axis)


def twice(table):
    zero = jnp.zeros_like(table)
    return jnp.concatenate(
        [jnp.concatenate([table, zero], axis=1), jnp.concatenate([zero, table], axis=1)], axis=0
    ).astype(jnp.bfloat16)


def along_x_table(blocks, cols_x):
    shape = (blocks * cols_x, blocks * cols_x)
    row, col = index(shape, 0), index(shape, 1)
    inside = lax.div(row, cols_x) == lax.div(col, cols_x)
    return jnp.where(inside, taps_at(col - row), 0.0).astype(jnp.bfloat16)


def along_z_table(cols_z):
    shape = (cols_z, cols_z)
    return twice(-taps_at(index(shape, 0) - index(shape, 1)))


def edge_z_table(cols_z):
    shape = (2 * GROUP, cols_z)
    row, col = index(shape, 0), index(shape, 1)
    ahead = jnp.where(row < REACH, taps_at(cols_z + row - col), 0.0)
    behind = jnp.where((row >= GROUP) & (row < GROUP + REACH), taps_at(row - GROUP - REACH - col), 0.0)
    return twice(-(ahead + behind))


def ends_z_table(cols_z):
    shape = (2 * GROUP, cols_z)
    row, col = index(shape, 0), index(shape, 1)
    ahead = (row < REACH) & (col == row)
    behind = (row >= GROUP) & (row < GROUP + REACH) & (col == cols_z - REACH + row - GROUP)
    return jnp.where(ahead | behind, 1.0, 0.0).astype(jnp.bfloat16)


def matmul(left, right, dims=None):
    dims = dims or (((1,), (0,)), ((), ()))
    return lax.dot_general(left, right, dims, preferred_element_type=jnp.float32)


def flat_rows(velocity, field, start, count):
    block = velocity[field, start : start + count]
    return block.reshape(-1, block.shape[-1])


def two_blocks(velocity, field, start):
    blocks = [flat_rows(velocity, field, start + at, FEW) for at in (0, FEW)]
    return jnp.concatenate(blocks, axis=1)


def sides_kernel(velocity, head, tail, first_rows, last_rows):
    reach, planes, snaps, cols_z = head.shape
    cols_x = velocity.shape[3]
    first_rows[...] = velocity[1, :, :, :GROUP].reshape(first_rows.shape).astype(jnp.float32)
    last_rows[...] = velocity[1, :, :, cols_x - GROUP :].reshape(last_rows.shape).astype(jnp.float32)
    stride = planes * GROUP
    for p in range(planes):
        for h in range(reach):
            at = p * GROUP + h
            head[h, p] = first_rows[pl.ds(at, snaps, stride=stride), :].astype(jnp.bfloat16)
            at = (p + 1) * GROUP - reach + h
            tail[h, p] = last_rows[pl.ds(at, snaps, stride=stride), :].astype(jnp.bfloat16)


def span_kernel(velocity, passed, head, tail, passed_on):
    snaps, planes, cols_x = velocity.shape[1:4]
    share = 2 * GROUP
    ends_z = ends_z_table(velocity.shape[4])
    passed_on[...] = passed[...]
    for start in range(0, snaps, share):
        span = slice(start * planes * cols_x, (start + share) * planes * cols_x)
        cols = matmul(ends_z, flat_rows(velocity, 0, start, share), NT).astype(jnp.bfloat16)
        head[:, span] = cols[:GROUP]
        tail[:, span] = cols[GROUP:]


def inner_kernel(velocity, out):
    planes, cols_x, cols_z = velocity.shape[2:]
    count = FEW * planes * cols_x
    along_x = along_x_table(FEW * planes, cols_x)
    along_z = along_z_table(cols_z)
    for q in range(velocity.shape[1] // (2 * FEW)):
        value = matmul(along_x, two_blocks(velocity, 1, 2 * FEW * q))
        value = value + matmul(two_blocks(velocity, 0, 2 * FEW * q), along_z)
        for half in range(2):
            at = (2 * q + half) * count
            out[at : at + count, :] = value[:, half * cols_z : (half + 1) * cols_z]


def gram_kernel(inner, left_w, right_w, left_u, right_u, place, vort, rows_out, work):
    lines, snaps, cols_z = vort.shape
    planes = left_w.shape[1]
    cols_x = lines // planes
    kept = place.shape[1]
    count = lines * GROUP
    edge_z = edge_z_table(cols_z)
    for q in range(snaps // (2 * GROUP)):
        spans = [slice((2 * q + half) * count, (2 * q + half + 1) * count) for half in range(2)]
        cols = jnp.concatenate([side[:, span] for span in spans for side in (right_u, left_u)], axis=0)
        value = matmul(cols, edge_z, TN)
        for half in range(2):
            work[spans[half], :] = inner[spans[half], :] + value[:, half * cols_z : (half + 1) * cols_z]
    gram = jnp.zeros((snaps + kept, snaps), jnp.float32)
    lane = lax.broadcasted_iota(jnp.int32, (kept, 2 * cols_z), 1).astype(jnp.float32)
    down = jnp.broadcast_to(place[...].astype(jnp.float32), (GROUP, kept)).T[:, :1]
    for pair in range(lines // 2):
        sides = []
        for line in (2 * pair, 2 * pair + 1):
            p, x = line // cols_x, line % cols_x
            value = work[pl.ds(line, snaps, stride=lines), :]
            for h in range(REACH):
                if tap(cols_x + h - x):
                    value = value + tap(cols_x + h - x) * right_w[h, p].astype(jnp.float32)
                if tap(h - REACH - x):
                    value = value + tap(h - REACH - x) * left_w[h, p].astype(jnp.float32)
            value = (value * (1.0 / TAP_SUM)).astype(jnp.bfloat16)
            vort[line] = value
            sides.append(value)
        both = jnp.concatenate(sides, axis=1)
        chosen = jnp.where(lane == down - float(2 * pair * cols_z), 1.0, 0.0).astype(jnp.bfloat16)
        gram = gram + matmul(jnp.concatenate([both, chosen], axis=0), both, NT)
    for part in range((snaps + kept) // kept):
        rows_out[:, 0, part * snaps : (part + 1) * snaps] = gram[part * kept : (part + 1) * kept]


def spread(tile, row):
    return jnp.broadcast_to(tile[row : row + 1], tile.shape)


def orthonormal_rows(block, inner):
    kept, snaps = block.shape
    shape = (GROUP, snaps)
    count = kept // GROUP
    row_at = index(shape, 0)
    inner = jnp.concatenate([inner, jnp.zeros((kept, snaps - kept), inner.dtype)], axis=1)
    inner_rows = [inner[GROUP * i : GROUP * (i + 1)] for i in range(count)]
    block_rows = [block[GROUP * i : GROUP * (i + 1)] for i in range(count)]
    for b in range(count):
        cols = []
        for t in range(GROUP):
            at = GROUP * b + t
            cols.append([jnp.broadcast_to(rows[:, at : at + 1], shape) for rows in inner_rows[b:]])
        pivot = [[spread(cols[t][0], i) for i in range(GROUP)] for t in range(GROUP)]
        cols = [col[1:] for col in cols]
        inner_at = [spread(inner_rows[b], t) for t in range(GROUP)]
        block_at = [spread(block_rows[b], t) for t in range(GROUP)]
        done = jnp.zeros(shape, jnp.float32)
        for t in range(GROUP):
            root = lax.rsqrt(pivot[t][t])
            inverse = root * root
            for later in range(t + 1, GROUP):
                part = pivot[t][later] * inverse
                for i in range(later, GROUP):
                    pivot[later][i] = pivot[later][i] - pivot[t][i] * part
                inner_at[later] = inner_at[later] - inner_at[t] * part
                block_at[later] = block_at[later] - block_at[t] * part
                cols[later] = [col - first * part for col, first in zip(cols[later], cols[t])]
            done = jnp.where(row_at == t, block_at[t] * root, done)
            inner_part = inner_at[t] * inverse
            block_part = block_at[t] * inverse
            for r in range(b + 1, count):
                inner_rows[r] = inner_rows[r] - cols[t][r - b - 1] * inner_part
                block_rows[r] = block_rows[r] - cols[t][r - b - 1] * block_part
        block_rows[b] = done
    return jnp.concatenate(block_rows, axis=0)


def modes_kernel(cells, rows, rank, start, vort, modes, basis, work):
    kept, snaps = start.shape
    lines = vort.shape[0]
    parts = [rows[:, 0, b * snaps : (b + 1) * snaps] for b in range(snaps // kept + 1)]
    gram = jnp.concatenate(parts[:-1], axis=0) * (1.0 / cells)
    picked = parts[-1]
    scale = jnp.where(rank[...] < kept, 1.0, 0.25).astype(jnp.float32)
    now = start[...]
    for step in range(ITERS):
        block = lax.dot_general(now * scale, gram, NT, precision=HIGHEST, preferred_element_type=jnp.float32)
        block = block * scale
        inner = lax.dot_general(block, block, NT, precision=HIGHEST, preferred_element_type=jnp.float32)
        now = orthonormal_rows(block, inner)
    coef = (now * scale).astype(jnp.bfloat16)
    anchor = jnp.sum(picked * coef.astype(jnp.float32), axis=1, keepdims=True)
    orient = anchor / jnp.maximum(jnp.abs(anchor), 1.0)
    basis[...] = now * orient
    for line in range(lines):
        work[pl.ds(line, kept, stride=lines), :] = matmul(coef, vort[line]) * orient
    modes[...] = work[...].astype(jnp.bfloat16).reshape(modes.shape)


def local_place(anchor_index, planes, cols_x, cols_z, total_x, total_z):
    plane_of = anchor_index // (total_x * total_z)
    remain = anchor_index % (total_x * total_z)
    local_x = remain // total_z - lax.axis_index("gx") * cols_x
    local_z = remain % total_z - lax.axis_index("gz") * cols_z
    owned = (local_x >= 0) & (local_x < cols_x) & (local_z >= 0) & (local_z < cols_z)
    return jnp.where(owned, (plane_of * cols_x + local_x) * cols_z + local_z, -1)


def shifted(value, axis, step):
    count = lax.axis_size(axis)
    return lax.ppermute(value, axis, [(i, (i + step) % count) for i in range(count)])


def exchanged(rows, axis):
    return lax.all_to_all(rows, axis, 0, 0, tiled=True)


def summed(rows, axis):
    count = lax.axis_size(axis)
    return jnp.sum(rows.reshape((count, rows.shape[0] // count) + rows.shape[1:]), axis=0)


def copies(rows, axis):
    return jnp.tile(rows, (lax.axis_size(axis),) + (1,) * (rows.ndim - 1))


def near(shape, dtype):
    return pltpu.VMEM(shape, dtype)


def local_call(kernel, outs, name, scratch=()):
    def run(*args):
        return pl.pallas_call(
            kernel,
            in_specs=[pl.BlockSpec(memory_space=pltpu.VMEM)] * len(args),
            out_specs=[pl.BlockSpec(memory_space=pltpu.VMEM)] * len(outs),
            out_shape=outs,
            scratch_shapes=list(scratch),
            compiler_params=pltpu.CompilerParams(vmem_limit_bytes=KERNEL_VMEM),
            name=name,
        )(*[pltpu.with_memory_space_constraint(arg, pltpu.VMEM) for arg in args])

    return run


def body(velocity, snapshot_rank, anchor_index, start_basis):
    _, snaps, planes, cols_x, cols_z = velocity.shape
    kept = start_basis.shape[1]
    lines = planes * cols_x
    total_x = cols_x * lax.axis_size("gx")
    total_z = cols_z * lax.axis_size("gz")
    side = near((REACH, planes, snaps, cols_z), jnp.bfloat16)
    strip = near((GROUP, snaps * lines), jnp.bfloat16)
    rows_at = pltpu.VMEM((snaps * planes * GROUP, cols_z), jnp.float32)
    head_w, tail_w = local_call(sides_kernel, [side, side], "sides", [rows_at] * 2)(velocity)
    left_w = shifted(tail_w, "gx", 1)
    head_u, tail_u, head_w = local_call(span_kernel, [strip, strip, side], "span")(velocity, head_w)
    right_w = shifted(head_w, "gx", -1)
    left_u = shifted(tail_u, "gz", 1)
    right_u = shifted(head_u, "gz", -1)
    field = near((snaps * lines, cols_z), jnp.float32)
    (inner,) = local_call(inner_kernel, [field], "inner")(velocity)
    place = local_place(anchor_index, planes, cols_x, cols_z, total_x, total_z)
    vort, rows = local_call(
        gram_kernel,
        [
            near((lines, snaps, cols_z), jnp.bfloat16),
            near((kept, 1, (snaps // kept + 1) * snaps), jnp.float32),
        ],
        "gram",
        [field],
    )(inner, left_w, right_w, left_u, right_u, place[None, :])
    mine = summed(exchanged(rows, "gx"), "gx")
    mine = summed(exchanged(copies(mine, "gz"), "gz"), "gz")
    rows = exchanged(copies(mine, "gx"), "gx")
    modes, basis = local_call(
        partial(modes_kernel, float(planes * total_x * total_z)),
        [
            jax.ShapeDtypeStruct((kept, planes, cols_x, cols_z), jnp.bfloat16),
            jax.ShapeDtypeStruct((kept, snaps), jnp.float32),
        ],
        "modes",
        [pltpu.VMEM((kept * lines, cols_z), jnp.float32)],
    )(rows, snapshot_rank[None, :], start_basis.T, vort)
    return modes, basis.T


def solution(mesh):
    return jax.shard_map(
        body,
        mesh=mesh,
        in_specs=(P(None, None, None, "gx", "gz"), P(), P(), P()),
        out_specs=(P(None, None, "gx", "gz"), P()),
        check_vma=False,
    )
```

```python
import math
from functools import partial

import jax
import jax.numpy as jnp
from jax import lax
from jax.experimental import pallas as pl
from jax.experimental.pallas import tpu as pltpu
from jax.sharding import PartitionSpec as P

ITERS = 3
CHIPS = "chips"
CORES = "cores"
GX = (CHIPS, CORES)
GZ = "gz"
REACH = 3
TAPS = (45.0, -9.0, 1.0)
TAP_SUM = 60.0
GROUP = 8
FEW = 4
PIECES = 16
KERNEL_VMEM = 16 << 20
HIGHEST = lax.Precision.HIGHEST
NT = (((1,), (1,)), ((), ()))
TN = (((0,), (0,)), ((), ()))


def tap(offset):
    size = abs(offset)
    if size < 1 or size > REACH:
        return 0.0
    return TAPS[size - 1] if offset > 0 else -TAPS[size - 1]


def taps_at(offset):
    value = jnp.zeros(offset.shape, jnp.float32)
    for size in range(1, REACH + 1):
        value = jnp.where(offset == size, TAPS[size - 1], value)
        value = jnp.where(offset == -size, -TAPS[size - 1], value)
    return value


def index(shape, axis):
    return lax.broadcasted_iota(jnp.int32, shape, axis)


def twice(table):
    zero = jnp.zeros_like(table)
    return jnp.concatenate(
        [jnp.concatenate([table, zero], axis=1), jnp.concatenate([zero, table], axis=1)], axis=0
    ).astype(jnp.bfloat16)


def along_x_table(blocks, cols_x):
    shape = (blocks * cols_x, blocks * cols_x)
    row, col = index(shape, 0), index(shape, 1)
    inside = lax.div(row, cols_x) == lax.div(col, cols_x)
    return jnp.where(inside, taps_at(col - row), 0.0).astype(jnp.bfloat16)


def along_z_table(cols_z):
    shape = (cols_z, cols_z)
    return twice(-taps_at(index(shape, 0) - index(shape, 1)))


def edge_z_table(cols_z):
    shape = (2 * GROUP, cols_z)
    row, col = index(shape, 0), index(shape, 1)
    ahead = jnp.where(row < REACH, taps_at(cols_z + row - col), 0.0)
    behind = jnp.where((row >= GROUP) & (row < GROUP + REACH), taps_at(row - GROUP - REACH - col), 0.0)
    return twice(-(ahead + behind))


def ends_z_table(cols_z):
    shape = (2 * GROUP, cols_z)
    row, col = index(shape, 0), index(shape, 1)
    ahead = (row < REACH) & (col == row)
    behind = (row >= GROUP) & (row < GROUP + REACH) & (col == cols_z - REACH + row - GROUP)
    return jnp.where(ahead | behind, 1.0, 0.0).astype(jnp.bfloat16)


def matmul(left, right, dims=None):
    dims = dims or (((1,), (0,)), ((), ()))
    return lax.dot_general(left, right, dims, preferred_element_type=jnp.float32)


def flat_rows(velocity, field, start, count):
    block = velocity[field, start : start + count]
    return block.reshape(-1, block.shape[-1])


def two_blocks(velocity, field, start):
    blocks = [flat_rows(velocity, field, start + at, FEW) for at in (0, FEW)]
    return jnp.concatenate(blocks, axis=1)


def sides_kernel(velocity, head, tail, first, last, first_rows, last_rows, landed):
    reach, planes, snaps, cols_z = head.shape
    cols_x = velocity.shape[3]
    first_copy = pltpu.make_async_copy(velocity.at[1, :, :, pl.ds(0, GROUP)], first, landed.at[0])
    last_copy = pltpu.make_async_copy(velocity.at[1, :, :, pl.ds(cols_x - GROUP, GROUP)], last, landed.at[1])
    first_copy.start()
    last_copy.start()
    stride = planes * GROUP
    last_start = GROUP - reach
    for copy, tiles, rows, side, start in (
        (first_copy, first, first_rows, head, 0),
        (last_copy, last, last_rows, tail, last_start),
    ):
        copy.wait()
        rows[...] = tiles[...].reshape(rows.shape).astype(jnp.float32)
        for p in range(planes):
            for h in range(reach):
                at = p * GROUP + start + h
                side[h, p] = rows[pl.ds(at, snaps, stride=stride), :].astype(jnp.bfloat16)


def span_kernel(velocity, passed, head, tail, passed_on):
    snaps, planes, cols_x = velocity.shape[1:4]
    share = 2 * GROUP
    ends_z = ends_z_table(velocity.shape[4])
    passed_on[...] = passed[...]
    for start in range(0, snaps, share):
        span = slice(start * planes * cols_x, (start + share) * planes * cols_x)
        cols = matmul(ends_z, flat_rows(velocity, 0, start, share), NT).astype(jnp.bfloat16)
        head[:, span] = cols[:GROUP]
        tail[:, span] = cols[GROUP:]


def inner_kernel(velocity, out):
    planes, cols_x, cols_z = velocity.shape[2:]
    count = FEW * planes * cols_x
    along_x = along_x_table(FEW * planes, cols_x)
    along_z = along_z_table(cols_z)
    for q in range(velocity.shape[1] // (2 * FEW)):
        value = matmul(along_x, two_blocks(velocity, 1, 2 * FEW * q))
        value = value + matmul(two_blocks(velocity, 0, 2 * FEW * q), along_z)
        for half in range(2):
            at = (2 * q + half) * count
            out[at : at + count, :] = value[:, half * cols_z : (half + 1) * cols_z]


def across_kernel(inner, left_u, right_u, out):
    cols_z = inner.shape[1]
    count = inner.shape[0] // PIECES
    edge_z = edge_z_table(cols_z)
    for q in range(PIECES // 2):
        spans = [slice((2 * q + half) * count, (2 * q + half + 1) * count) for half in range(2)]
        cols = jnp.concatenate([side[:, span] for span in spans for side in (right_u, left_u)], axis=0)
        value = matmul(cols, edge_z, TN)
        for half in range(2):
            out[spans[half], :] = inner[spans[half], :] + value[:, half * cols_z : (half + 1) * cols_z]


def gram_kernel(inner, left_w, right_w, place, vort, rows_out):
    lines, snaps, cols_z = vort.shape
    planes = left_w.shape[1]
    cols_x = lines // planes
    kept = place.shape[1]
    gram = jnp.zeros((snaps + kept, snaps), jnp.float32)
    lane = lax.broadcasted_iota(jnp.int32, (kept, 2 * cols_z), 1).astype(jnp.float32)
    down = jnp.broadcast_to(place[...].astype(jnp.float32), (GROUP, kept)).T[:, :1]
    for pair in range(lines // 2):
        sides = []
        for line in (2 * pair, 2 * pair + 1):
            p, x = line // cols_x, line % cols_x
            value = inner[pl.ds(line, snaps, stride=lines), :]
            for h in range(REACH):
                if tap(cols_x + h - x):
                    value = value + tap(cols_x + h - x) * right_w[h, p].astype(jnp.float32)
                if tap(h - REACH - x):
                    value = value + tap(h - REACH - x) * left_w[h, p].astype(jnp.float32)
            value = (value * (1.0 / TAP_SUM)).astype(jnp.bfloat16)
            vort[line] = value
            sides.append(value)
        both = jnp.concatenate(sides, axis=1)
        chosen = jnp.where(lane == down - float(2 * pair * cols_z), 1.0, 0.0).astype(jnp.bfloat16)
        gram = gram + matmul(jnp.concatenate([both, chosen], axis=0), both, NT)
    for part in range((snaps + kept) // kept):
        rows_out[:, 0, part * snaps : (part + 1) * snaps] = gram[part * kept : (part + 1) * kept]


def spread(tile, row):
    return jnp.broadcast_to(tile[row : row + 1], tile.shape)


def orthonormal_rows(block, inner):
    kept, snaps = block.shape
    shape = (GROUP, snaps)
    count = kept // GROUP
    row_at = index(shape, 0)
    inner = jnp.concatenate([inner, jnp.zeros((kept, snaps - kept), inner.dtype)], axis=1)
    inner_rows = [inner[GROUP * i : GROUP * (i + 1)] for i in range(count)]
    block_rows = [block[GROUP * i : GROUP * (i + 1)] for i in range(count)]
    for b in range(count):
        cols = []
        for t in range(GROUP):
            at = GROUP * b + t
            cols.append([jnp.broadcast_to(rows[:, at : at + 1], shape) for rows in inner_rows[b:]])
        pivot = [[spread(cols[t][0], i) for i in range(GROUP)] for t in range(GROUP)]
        cols = [col[1:] for col in cols]
        inner_at = [spread(inner_rows[b], t) for t in range(GROUP)]
        block_at = [spread(block_rows[b], t) for t in range(GROUP)]
        done = jnp.zeros(shape, jnp.float32)
        for t in range(GROUP):
            root = lax.rsqrt(pivot[t][t])
            inverse = root * root
            for later in range(t + 1, GROUP):
                part = pivot[t][later] * inverse
                for i in range(later, GROUP):
                    pivot[later][i] = pivot[later][i] - pivot[t][i] * part
                inner_at[later] = inner_at[later] - inner_at[t] * part
                block_at[later] = block_at[later] - block_at[t] * part
                cols[later] = [col - first * part for col, first in zip(cols[later], cols[t])]
            done = jnp.where(row_at == t, block_at[t] * root, done)
            inner_part = inner_at[t] * inverse
            block_part = block_at[t] * inverse
            for r in range(b + 1, count):
                inner_rows[r] = inner_rows[r] - cols[t][r - b - 1] * inner_part
                block_rows[r] = block_rows[r] - cols[t][r - b - 1] * block_part
        block_rows[b] = done
    return jnp.concatenate(block_rows, axis=0)


def modes_kernel(cells, rows, rank, start, vort, modes, basis, work):
    kept, snaps = start.shape
    lines = vort.shape[0]
    parts = [rows[:, 0, b * snaps : (b + 1) * snaps] for b in range(snaps // kept + 1)]
    gram = jnp.concatenate(parts[:-1], axis=0) * (1.0 / cells)
    picked = parts[-1]
    scale = jnp.where(rank[...] < kept, 1.0, 0.25).astype(jnp.float32)
    now = start[...]
    for step in range(ITERS):
        block = lax.dot_general(now * scale, gram, NT, precision=HIGHEST, preferred_element_type=jnp.float32)
        block = block * scale
        inner = lax.dot_general(block, block, NT, precision=HIGHEST, preferred_element_type=jnp.float32)
        now = orthonormal_rows(block, inner)
    coef = (now * scale).astype(jnp.bfloat16)
    anchor = jnp.sum(picked * coef.astype(jnp.float32), axis=1, keepdims=True)
    orient = anchor / jnp.maximum(jnp.abs(anchor), 1.0)
    basis[...] = now * orient
    for line in range(lines):
        work[pl.ds(line, kept, stride=lines), :] = matmul(coef, vort[line]) * orient
    modes[...] = work[...].astype(jnp.bfloat16).reshape(modes.shape)


def local_place(anchor_index, planes, cols_x, cols_z, total_x, total_z):
    plane_of = anchor_index // (total_x * total_z)
    remain = anchor_index % (total_x * total_z)
    local_x = remain // total_z - lax.axis_index(GX) * cols_x
    local_z = remain % total_z - lax.axis_index(GZ) * cols_z
    owned = (local_x >= 0) & (local_x < cols_x) & (local_z >= 0) & (local_z < cols_z)
    return jnp.where(owned, (plane_of * cols_x + local_x) * cols_z + local_z, -1)


def size_of(axes):
    return math.prod(lax.axis_size(axis) for axis in ((axes,) if isinstance(axes, str) else axes))


def shifted(value, axis, step):
    count = size_of(axis)
    return lax.ppermute(value, axis, [(i, (i + step) % count) for i in range(count)])


def exchanged(rows, axis):
    return lax.all_to_all(rows, axis, 0, 0, tiled=True)


def summed(rows, axis):
    count = size_of(axis)
    return jnp.sum(rows.reshape((count, rows.shape[0] // count) + rows.shape[1:]), axis=0)


def copies(rows, axis):
    return jnp.tile(rows, (size_of(axis),) + (1,) * (rows.ndim - 1))


def near(shape, dtype):
    return pltpu.VMEM(shape, dtype)


def local_call(kernel, outs, name, scratch=(), space=pltpu.VMEM):
    def run(*args):
        return pl.pallas_call(
            kernel,
            in_specs=[pl.BlockSpec(memory_space=space)] * len(args),
            out_specs=[pl.BlockSpec(memory_space=pltpu.VMEM)] * len(outs),
            out_shape=outs,
            scratch_shapes=list(scratch),
            compiler_params=pltpu.CompilerParams(vmem_limit_bytes=KERNEL_VMEM),
            name=name,
        )(*[pltpu.with_memory_space_constraint(arg, space) for arg in args])

    return run


def body(velocity, snapshot_rank, anchor_index, start_basis):
    _, snaps, planes, cols_x, cols_z = velocity.shape
    kept = start_basis.shape[1]
    lines = planes * cols_x
    total_x = cols_x * size_of(GX)
    total_z = cols_z * size_of(GZ)
    side = near((REACH, planes, snaps, cols_z), jnp.bfloat16)
    strip = near((GROUP, snaps * lines), jnp.bfloat16)
    rows_at = pltpu.VMEM((snaps * planes * GROUP, cols_z), jnp.float32)
    tiles = pltpu.VMEM((snaps, planes, GROUP, cols_z), jnp.bfloat16)
    scratch = [tiles, tiles, rows_at, rows_at, pltpu.SemaphoreType.DMA((2,))]
    head_w, tail_w = local_call(sides_kernel, [side, side], "sides", scratch, pltpu.HBM)(velocity)
    left_w = shifted(tail_w, GX, 1)
    head_u, tail_u, head_w = local_call(span_kernel, [strip, strip, side], "span")(velocity, head_w)
    right_w = shifted(head_w, GX, -1)
    left_u = shifted(tail_u, GZ, 1)
    right_u = shifted(head_u, GZ, -1)
    field = near((snaps * lines, cols_z), jnp.float32)
    (inner,) = local_call(inner_kernel, [field], "inner")(velocity)
    (inner,) = local_call(across_kernel, [field], "across")(inner, left_u, right_u)
    place = local_place(anchor_index, planes, cols_x, cols_z, total_x, total_z)
    vort, rows = local_call(
        gram_kernel,
        [
            near((lines, snaps, cols_z), jnp.bfloat16),
            near((kept, 1, (snaps // kept + 1) * snaps), jnp.float32),
        ],
        "gram",
    )(inner, left_w, right_w, place[None, :])
    mine = summed(exchanged(rows, CHIPS), CHIPS)
    mine = summed(exchanged(copies(mine, (CORES, GZ)), (CORES, GZ)), (CORES, GZ))
    rows = exchanged(copies(mine, CHIPS), CHIPS)
    modes, basis = local_call(
        partial(modes_kernel, float(planes * total_x * total_z)),
        [
            jax.ShapeDtypeStruct((kept, planes, cols_x, cols_z), jnp.bfloat16),
            jax.ShapeDtypeStruct((kept, snaps), jnp.float32),
        ],
        "modes",
        [pltpu.VMEM((kept * lines, cols_z), jnp.float32)],
    )(rows, snapshot_rank[None, :], start_basis.T, vort)
    return modes, basis.T


def solution(mesh):
    count_x, count_z = mesh.shape["gx"], mesh.shape["gz"]
    split = jax.sharding.Mesh(mesh.devices.reshape(count_x // 2, 2, count_z), (CHIPS, CORES, GZ))
    return jax.shard_map(
        body,
        mesh=split,
        in_specs=(P(None, None, None, GX, GZ), P(), P(), P()),
        out_specs=(P(None, None, GX, GZ), P()),
        check_vma=False,
    )
```

```python
import math
from functools import partial

import jax
import jax.numpy as jnp
from jax import lax
from jax.experimental import pallas as pl
from jax.experimental.pallas import tpu as pltpu
from jax.sharding import PartitionSpec as P

ITERS = 3
CHIPS = "chips"
CORES = "cores"
GX = (CHIPS, CORES)
GZ = "gz"
REACH = 3
TAPS = (45.0, -9.0, 1.0)
TAP_SUM = 60.0
GROUP = 8
FEW = 4
PIECES = 16
LOADS = 2
KERNEL_VMEM = 16 << 20
HIGHEST = lax.Precision.HIGHEST
NT = (((1,), (1,)), ((), ()))
TN = (((0,), (0,)), ((), ()))


def tap(offset):
    size = abs(offset)
    if size < 1 or size > REACH:
        return 0.0
    return TAPS[size - 1] if offset > 0 else -TAPS[size - 1]


def taps_at(offset):
    value = jnp.zeros(offset.shape, jnp.float32)
    for size in range(1, REACH + 1):
        value = jnp.where(offset == size, TAPS[size - 1], value)
        value = jnp.where(offset == -size, -TAPS[size - 1], value)
    return value


def index(shape, axis):
    return lax.broadcasted_iota(jnp.int32, shape, axis)


def twice(table):
    zero = jnp.zeros_like(table)
    return jnp.concatenate(
        [jnp.concatenate([table, zero], axis=1), jnp.concatenate([zero, table], axis=1)], axis=0
    ).astype(jnp.bfloat16)


def along_x_table(blocks, cols_x):
    shape = (blocks * cols_x, blocks * cols_x)
    row, col = index(shape, 0), index(shape, 1)
    inside = lax.div(row, cols_x) == lax.div(col, cols_x)
    return jnp.where(inside, taps_at(col - row), 0.0).astype(jnp.bfloat16)


def along_z_table(cols_z):
    shape = (cols_z, cols_z)
    return twice(-taps_at(index(shape, 0) - index(shape, 1)))


def edge_z_table(cols_z):
    shape = (2 * GROUP, cols_z)
    row, col = index(shape, 0), index(shape, 1)
    ahead = jnp.where(row < REACH, taps_at(cols_z + row - col), 0.0)
    behind = jnp.where((row >= GROUP) & (row < GROUP + REACH), taps_at(row - GROUP - REACH - col), 0.0)
    return twice(-(ahead + behind))


def ends_z_table(cols_z):
    shape = (2 * GROUP, cols_z)
    row, col = index(shape, 0), index(shape, 1)
    ahead = (row < REACH) & (col == row)
    behind = (row >= GROUP) & (row < GROUP + REACH) & (col == cols_z - REACH + row - GROUP)
    return jnp.where(ahead | behind, 1.0, 0.0).astype(jnp.bfloat16)


def matmul(left, right, dims=None):
    dims = dims or (((1,), (0,)), ((), ()))
    return lax.dot_general(left, right, dims, preferred_element_type=jnp.float32)


def flat_rows(field, start, count):
    block = field[start : start + count]
    return block.reshape(-1, block.shape[-1])


def two_blocks(field, start):
    return jnp.concatenate([flat_rows(field, start + at, FEW) for at in (0, FEW)], axis=1)


def ends_kernel(velocity, head_w, tail_w, head_u, tail_u, wide, long, first_rows, last_rows, landed):
    reach, planes, snaps, cols_z = head_w.shape
    cols_x = wide.shape[2]
    share = snaps // LOADS
    loads = []
    for field, near_field in ((1, wide), (0, long)):
        for part in range(LOADS):
            here = pl.ds(part * share, share)
            source = velocity.at[field, here]
            loads.append(pltpu.make_async_copy(source, near_field.at[here], landed.at[len(loads)]))
            loads[-1].start()
    stride = planes * GROUP
    for part in range(LOADS):
        loads[part].wait()
        here = slice(part * share, (part + 1) * share)
        rows = slice(part * share * stride, (part + 1) * share * stride)
        size = (share * stride, cols_z)
        first_rows[rows, :] = wide[here, :, :GROUP].reshape(size).astype(jnp.float32)
        last_rows[rows, :] = wide[here, :, cols_x - GROUP :].reshape(size).astype(jnp.float32)
        for p in range(planes):
            for h in range(reach):
                at = part * share * stride + p * GROUP + h
                head_w[h, p, here, :] = first_rows[pl.ds(at, share, stride=stride), :].astype(jnp.bfloat16)
                at = at + GROUP - reach
                tail_w[h, p, here, :] = last_rows[pl.ds(at, share, stride=stride), :].astype(jnp.bfloat16)
    ends_z = ends_z_table(cols_z)
    few = 2 * GROUP
    for part in range(LOADS):
        loads[LOADS + part].wait()
        for start in range(part * share, (part + 1) * share, few):
            span = slice(start * planes * cols_x, (start + few) * planes * cols_x)
            cols = matmul(ends_z, flat_rows(long, start, few), NT).astype(jnp.bfloat16)
            head_u[:, span] = cols[:GROUP]
            tail_u[:, span] = cols[GROUP:]


def inner_kernel(long, wide, out):
    planes, cols_x, cols_z = wide.shape[1:]
    count = FEW * planes * cols_x
    along_x = along_x_table(FEW * planes, cols_x)
    along_z = along_z_table(cols_z)
    for q in range(wide.shape[0] // (2 * FEW)):
        value = matmul(along_x, two_blocks(wide, 2 * FEW * q))
        value = value + matmul(two_blocks(long, 2 * FEW * q), along_z)
        for half in range(2):
            at = (2 * q + half) * count
            out[at : at + count, :] = value[:, half * cols_z : (half + 1) * cols_z]


def across_kernel(inner, left_u, right_u, out):
    cols_z = inner.shape[1]
    count = inner.shape[0] // PIECES
    edge_z = edge_z_table(cols_z)
    for q in range(PIECES // 2):
        spans = [slice((2 * q + half) * count, (2 * q + half + 1) * count) for half in range(2)]
        cols = jnp.concatenate([side[:, span] for span in spans for side in (right_u, left_u)], axis=0)
        value = matmul(cols, edge_z, TN)
        for half in range(2):
            out[spans[half], :] = inner[spans[half], :] + value[:, half * cols_z : (half + 1) * cols_z]


def inside_lines(planes, cols_x):
    return [p * cols_x + x for p in range(planes) for x in range(REACH, cols_x - REACH)]


def outside_lines(planes, cols_x):
    inside = set(inside_lines(planes, cols_x))
    return [line for line in range(planes * cols_x) if line not in inside]


def gram_of(lines, vorticity, place, vort):
    _, snaps, cols_z = vort.shape
    kept = place.shape[1]
    gram = jnp.zeros((snaps + kept, snaps), jnp.float32)
    lane = index((kept, 2 * cols_z), 1)
    down = jnp.broadcast_to(place[...].astype(jnp.float32), (GROUP, kept)).T[:, :1]
    for at in range(0, len(lines), 2):
        both = []
        for line in lines[at : at + 2]:
            value = (vorticity(line) * (1.0 / TAP_SUM)).astype(jnp.bfloat16)
            vort[at + len(both)] = value
            both.append(value)
        both = jnp.concatenate(both, axis=1)
        cell = lane + jnp.where(lane < cols_z, lines[at] * cols_z, (lines[at + 1] - 1) * cols_z)
        chosen = jnp.where(cell.astype(jnp.float32) == down, 1.0, 0.0).astype(jnp.bfloat16)
        gram = gram + matmul(jnp.concatenate([both, chosen], axis=0), both, NT)
    return gram


def inside_kernel(planes, inner, place, vort, partial_gram):
    snaps = vort.shape[1]
    lines = inner.shape[0] // snaps
    vorticity = lambda line: inner[pl.ds(line, snaps, stride=lines), :]
    partial_gram[...] = gram_of(inside_lines(planes, lines // planes), vorticity, place, vort)


def outside_kernel(inner, left_w, right_w, place, partial_gram, vort, rows_out):
    snaps = vort.shape[1]
    planes = left_w.shape[1]
    lines = inner.shape[0] // snaps
    cols_x = lines // planes
    kept = place.shape[1]

    def vorticity(line):
        p, x = line // cols_x, line % cols_x
        value = inner[pl.ds(line, snaps, stride=lines), :]
        for h in range(REACH):
            if tap(cols_x + h - x):
                value = value + tap(cols_x + h - x) * right_w[h, p].astype(jnp.float32)
            if tap(h - REACH - x):
                value = value + tap(h - REACH - x) * left_w[h, p].astype(jnp.float32)
        return value

    gram = partial_gram[...] + gram_of(outside_lines(planes, cols_x), vorticity, place, vort)
    for part in range((snaps + kept) // kept):
        rows_out[:, 0, part * snaps : (part + 1) * snaps] = gram[part * kept : (part + 1) * kept]


def spread(tile, row):
    return jnp.broadcast_to(tile[row : row + 1], tile.shape)


def orthonormal_rows(block, inner):
    kept, snaps = block.shape
    shape = (GROUP, snaps)
    count = kept // GROUP
    row_at = index(shape, 0)
    inner = jnp.concatenate([inner, jnp.zeros((kept, snaps - kept), inner.dtype)], axis=1)
    inner_rows = [inner[GROUP * i : GROUP * (i + 1)] for i in range(count)]
    block_rows = [block[GROUP * i : GROUP * (i + 1)] for i in range(count)]
    for b in range(count):
        cols = []
        for t in range(GROUP):
            at = GROUP * b + t
            cols.append([jnp.broadcast_to(rows[:, at : at + 1], shape) for rows in inner_rows[b:]])
        pivot = [[spread(cols[t][0], i) for i in range(GROUP)] for t in range(GROUP)]
        cols = [col[1:] for col in cols]
        inner_at = [spread(inner_rows[b], t) for t in range(GROUP)]
        block_at = [spread(block_rows[b], t) for t in range(GROUP)]
        done = jnp.zeros(shape, jnp.float32)
        for t in range(GROUP):
            root = lax.rsqrt(pivot[t][t])
            inverse = root * root
            for later in range(t + 1, GROUP):
                part = pivot[t][later] * inverse
                for i in range(later, GROUP):
                    pivot[later][i] = pivot[later][i] - pivot[t][i] * part
                inner_at[later] = inner_at[later] - inner_at[t] * part
                block_at[later] = block_at[later] - block_at[t] * part
                cols[later] = [col - first * part for col, first in zip(cols[later], cols[t])]
            done = jnp.where(row_at == t, block_at[t] * root, done)
            inner_part = inner_at[t] * inverse
            block_part = block_at[t] * inverse
            for r in range(b + 1, count):
                inner_rows[r] = inner_rows[r] - cols[t][r - b - 1] * inner_part
                block_rows[r] = block_rows[r] - cols[t][r - b - 1] * block_part
        block_rows[b] = done
    return jnp.concatenate(block_rows, axis=0)


def modes_kernel(cells, rows, rank, start, vort_in, vort_out, modes, basis, work):
    kept, snaps = start.shape
    planes, cols_x = modes.shape[1:3]
    lines = planes * cols_x
    parts = [rows[:, 0, b * snaps : (b + 1) * snaps] for b in range(snaps // kept + 1)]
    gram = jnp.concatenate(parts[:-1], axis=0) * (1.0 / cells)
    picked = parts[-1]
    scale = jnp.where(rank[...] < kept, 1.0, 0.25).astype(jnp.float32)
    now = start[...]
    for step in range(ITERS):
        block = lax.dot_general(now * scale, gram, NT, precision=HIGHEST, preferred_element_type=jnp.float32)
        block = block * scale
        inner = lax.dot_general(block, block, NT, precision=HIGHEST, preferred_element_type=jnp.float32)
        now = orthonormal_rows(block, inner)
    coef = (now * scale).astype(jnp.bfloat16)
    anchor = jnp.sum(picked * coef.astype(jnp.float32), axis=1, keepdims=True)
    orient = anchor / jnp.maximum(jnp.abs(anchor), 1.0)
    basis[...] = now * orient
    for vort, held in (
        (vort_in, inside_lines(planes, cols_x)),
        (vort_out, outside_lines(planes, cols_x)),
    ):
        for at, line in enumerate(held):
            work[pl.ds(line, kept, stride=lines), :] = matmul(coef, vort[at]) * orient
    modes[...] = work[...].astype(jnp.bfloat16).reshape(modes.shape)


def local_place(anchor_index, planes, cols_x, cols_z, total_x, total_z):
    plane_of = anchor_index // (total_x * total_z)
    remain = anchor_index % (total_x * total_z)
    local_x = remain // total_z - lax.axis_index(GX) * cols_x
    local_z = remain % total_z - lax.axis_index(GZ) * cols_z
    owned = (local_x >= 0) & (local_x < cols_x) & (local_z >= 0) & (local_z < cols_z)
    return jnp.where(owned, (plane_of * cols_x + local_x) * cols_z + local_z, -1)


def size_of(axes):
    return math.prod(lax.axis_size(axis) for axis in ((axes,) if isinstance(axes, str) else axes))


def shifted(value, axis, step):
    count = size_of(axis)
    return lax.ppermute(value, axis, [(i, (i + step) % count) for i in range(count)])


def exchanged(rows, axis):
    return lax.all_to_all(rows, axis, 0, 0, tiled=True)


def summed(rows, axis):
    count = size_of(axis)
    return jnp.sum(rows.reshape((count, rows.shape[0] // count) + rows.shape[1:]), axis=0)


def copies(rows, axis):
    return jnp.tile(rows, (size_of(axis),) + (1,) * (rows.ndim - 1))


def near(shape, dtype):
    return pltpu.VMEM(shape, dtype)


def local_call(kernel, outs, name, scratch=(), space=pltpu.VMEM):
    def run(*args):
        return pl.pallas_call(
            kernel,
            in_specs=[pl.BlockSpec(memory_space=space)] * len(args),
            out_specs=[pl.BlockSpec(memory_space=pltpu.VMEM)] * len(outs),
            out_shape=outs,
            scratch_shapes=list(scratch),
            compiler_params=pltpu.CompilerParams(vmem_limit_bytes=KERNEL_VMEM),
            name=name,
        )(*[pltpu.with_memory_space_constraint(arg, space) for arg in args])

    return run


def body(velocity, snapshot_rank, anchor_index, start_basis):
    _, snaps, planes, cols_x, cols_z = velocity.shape
    kept = start_basis.shape[1]
    lines = planes * cols_x
    total_x = cols_x * size_of(GX)
    total_z = cols_z * size_of(GZ)
    side = near((REACH, planes, snaps, cols_z), jnp.bfloat16)
    strip = near((GROUP, snaps * lines), jnp.bfloat16)
    rows_at = pltpu.VMEM((snaps * planes * GROUP, cols_z), jnp.float32)
    local = near((snaps, planes, cols_x, cols_z), jnp.bfloat16)
    head_w, tail_w, head_u, tail_u, wide, long = local_call(
        ends_kernel,
        [side, side, strip, strip, local, local],
        "ends",
        [rows_at, rows_at, pltpu.SemaphoreType.DMA((2 * LOADS,))],
        pltpu.HBM,
    )(velocity)
    left_w = shifted(tail_w, GX, 1)
    right_w = shifted(head_w, GX, -1)
    left_u = shifted(tail_u, GZ, 1)
    right_u = shifted(head_u, GZ, -1)
    field = near((snaps * lines, cols_z), jnp.float32)
    (inner,) = local_call(inner_kernel, [field], "inner")(long, wide)
    (inner,) = local_call(across_kernel, [field], "across")(inner, left_u, right_u)
    place = local_place(anchor_index, planes, cols_x, cols_z, total_x, total_z)
    within = len(inside_lines(planes, cols_x))
    vort_in, partial_gram = local_call(
        partial(inside_kernel, planes),
        [near((within, snaps, cols_z), jnp.bfloat16), near((snaps + kept, snaps), jnp.float32)],
        "inside",
    )(inner, place[None, :])
    vort_out, rows = local_call(
        outside_kernel,
        [
            near((lines - within, snaps, cols_z), jnp.bfloat16),
            near((kept, 1, (snaps // kept + 1) * snaps), jnp.float32),
        ],
        "outside",
    )(inner, left_w, right_w, place[None, :], partial_gram)
    mine = summed(exchanged(rows, CHIPS), CHIPS)
    mine = summed(exchanged(copies(mine, (CORES, GZ)), (CORES, GZ)), (CORES, GZ))
    rows = exchanged(copies(mine, CHIPS), CHIPS)
    modes, basis = local_call(
        partial(modes_kernel, float(planes * total_x * total_z)),
        [
            jax.ShapeDtypeStruct((kept, planes, cols_x, cols_z), jnp.bfloat16),
            jax.ShapeDtypeStruct((kept, snaps), jnp.float32),
        ],
        "modes",
        [pltpu.VMEM((kept * lines, cols_z), jnp.float32)],
    )(rows, snapshot_rank[None, :], start_basis.T, vort_in, vort_out)
    return modes, basis.T


def solution(mesh):
    count_x, count_z = mesh.shape["gx"], mesh.shape["gz"]
    split = jax.sharding.Mesh(mesh.devices.reshape(count_x // 2, 2, count_z), (CHIPS, CORES, GZ))
    return jax.shard_map(
        body,
        mesh=split,
        in_specs=(P(None, None, None, GX, GZ), P(), P(), P()),
        out_specs=(P(None, None, GX, GZ), P()),
        check_vma=False,
    )
```

```python
import math
from functools import partial

import jax
import jax.numpy as jnp
from jax import lax
from jax.experimental import pallas as pl
from jax.experimental.pallas import tpu as pltpu
from jax.sharding import PartitionSpec as P

ITERS = 3
CHIPS = "chips"
CORES = "cores"
GX = (CHIPS, CORES)
GZ = "gz"
REACH = 3
TAPS = (45.0, -9.0, 1.0)
TAP_SUM = 60.0
GROUP = 8
FEW = 4
PIECES = 16
LOADS = 2
KERNEL_VMEM = 16 << 20
HIGHEST = lax.Precision.HIGHEST
NT = (((1,), (1,)), ((), ()))
TN = (((0,), (0,)), ((), ()))


def tap(offset):
    size = abs(offset)
    if size < 1 or size > REACH:
        return 0.0
    return TAPS[size - 1] if offset > 0 else -TAPS[size - 1]


def taps_at(offset):
    value = jnp.zeros(offset.shape, jnp.float32)
    for size in range(1, REACH + 1):
        value = jnp.where(offset == size, TAPS[size - 1], value)
        value = jnp.where(offset == -size, -TAPS[size - 1], value)
    return value


def index(shape, axis):
    return lax.broadcasted_iota(jnp.int32, shape, axis)


def twice(table):
    zero = jnp.zeros_like(table)
    return jnp.concatenate(
        [jnp.concatenate([table, zero], axis=1), jnp.concatenate([zero, table], axis=1)], axis=0
    ).astype(jnp.bfloat16)


def along_x_table(blocks, cols_x):
    shape = (blocks * cols_x, blocks * cols_x)
    row, col = index(shape, 0), index(shape, 1)
    inside = lax.div(row, cols_x) == lax.div(col, cols_x)
    return jnp.where(inside, taps_at(col - row), 0.0).astype(jnp.bfloat16)


def along_z_table(cols_z):
    shape = (cols_z, cols_z)
    return twice(-taps_at(index(shape, 0) - index(shape, 1)))


def edge_z_table(cols_z):
    shape = (2 * GROUP, cols_z)
    row, col = index(shape, 0), index(shape, 1)
    ahead = jnp.where(row < REACH, taps_at(cols_z + row - col), 0.0)
    behind = jnp.where((row >= GROUP) & (row < GROUP + REACH), taps_at(row - GROUP - REACH - col), 0.0)
    return twice(-(ahead + behind))


def ends_z_table(cols_z):
    shape = (2 * GROUP, cols_z)
    row, col = index(shape, 0), index(shape, 1)
    ahead = (row < REACH) & (col == row)
    behind = (row >= GROUP) & (row < GROUP + REACH) & (col == cols_z - REACH + row - GROUP)
    return jnp.where(ahead | behind, 1.0, 0.0).astype(jnp.bfloat16)


def matmul(left, right, dims=None):
    dims = dims or (((1,), (0,)), ((), ()))
    return lax.dot_general(left, right, dims, preferred_element_type=jnp.float32)


def flat_rows(field, start, count):
    block = field[start : start + count]
    return block.reshape(-1, block.shape[-1])


def two_blocks(field, start):
    return jnp.concatenate([flat_rows(field, start + at, FEW) for at in (0, FEW)], axis=1)


def ends_kernel(velocity, head_w, tail_w, head_u, tail_u, wide, long, first_rows, last_rows, landed):
    reach, planes, snaps, cols_z = head_w.shape
    cols_x = wide.shape[2]
    share = snaps // LOADS
    loads = []
    for field, near_field in ((1, wide), (0, long)):
        for part in range(LOADS):
            here = pl.ds(part * share, share)
            source = velocity.at[field, here]
            loads.append(pltpu.make_async_copy(source, near_field.at[here], landed.at[len(loads)]))
            loads[-1].start()
    stride = planes * GROUP
    for part in range(LOADS):
        loads[part].wait()
        here = slice(part * share, (part + 1) * share)
        rows = slice(part * share * stride, (part + 1) * share * stride)
        size = (share * stride, cols_z)
        first_rows[rows, :] = wide[here, :, :GROUP].reshape(size).astype(jnp.float32)
        last_rows[rows, :] = wide[here, :, cols_x - GROUP :].reshape(size).astype(jnp.float32)
        for p in range(planes):
            for h in range(reach):
                at = part * share * stride + p * GROUP + h
                head_w[h, p, here, :] = first_rows[pl.ds(at, share, stride=stride), :].astype(jnp.bfloat16)
                at = at + GROUP - reach
                tail_w[h, p, here, :] = last_rows[pl.ds(at, share, stride=stride), :].astype(jnp.bfloat16)
    ends_z = ends_z_table(cols_z)
    few = 2 * GROUP
    for part in range(LOADS):
        loads[LOADS + part].wait()
        for start in range(part * share, (part + 1) * share, few):
            span = slice(start * planes * cols_x, (start + few) * planes * cols_x)
            cols = matmul(ends_z, flat_rows(long, start, few), NT).astype(jnp.bfloat16)
            head_u[:, span] = cols[:GROUP]
            tail_u[:, span] = cols[GROUP:]


def inner_kernel(long, wide, out):
    planes, cols_x, cols_z = wide.shape[1:]
    count = FEW * planes * cols_x
    along_x = along_x_table(FEW * planes, cols_x)
    along_z = along_z_table(cols_z)
    for q in range(wide.shape[0] // (2 * FEW)):
        value = matmul(along_x, two_blocks(wide, 2 * FEW * q))
        value = value + matmul(two_blocks(long, 2 * FEW * q), along_z)
        for half in range(2):
            at = (2 * q + half) * count
            out[at : at + count, :] = value[:, half * cols_z : (half + 1) * cols_z]


def across_kernel(inner, left_u, right_u, out):
    cols_z = inner.shape[1]
    count = inner.shape[0] // PIECES
    edge_z = edge_z_table(cols_z)
    for q in range(PIECES // 2):
        spans = [slice((2 * q + half) * count, (2 * q + half + 1) * count) for half in range(2)]
        cols = jnp.concatenate([side[:, span] for span in spans for side in (right_u, left_u)], axis=0)
        value = matmul(cols, edge_z, TN)
        for half in range(2):
            out[spans[half], :] = inner[spans[half], :] + value[:, half * cols_z : (half + 1) * cols_z]


def inside_lines(planes, cols_x):
    return [p * cols_x + x for p in range(planes) for x in range(REACH, cols_x - REACH)]


def outside_lines(planes, cols_x):
    inside = set(inside_lines(planes, cols_x))
    return [line for line in range(planes * cols_x) if line not in inside]


def gram_of(lines, vorticity, place, vort):
    _, snaps, cols_z = vort.shape
    kept = place.shape[1]
    gram = jnp.zeros((snaps + kept, snaps), jnp.float32)
    lane = index((kept, 2 * cols_z), 1)
    down = jnp.broadcast_to(place[...].astype(jnp.float32), (GROUP, kept)).T[:, :1]
    for at in range(0, len(lines), 2):
        both = []
        for line in lines[at : at + 2]:
            value = (vorticity(line) * (1.0 / TAP_SUM)).astype(jnp.bfloat16)
            vort[at + len(both)] = value
            both.append(value)
        both = jnp.concatenate(both, axis=1)
        cell = lane + jnp.where(lane < cols_z, lines[at] * cols_z, (lines[at + 1] - 1) * cols_z)
        chosen = jnp.where(cell.astype(jnp.float32) == down, 1.0, 0.0).astype(jnp.bfloat16)
        gram = gram + matmul(jnp.concatenate([both, chosen], axis=0), both, NT)
    return gram


def inside_kernel(planes, inner, place, vort, partial_gram):
    snaps = vort.shape[1]
    lines = inner.shape[0] // snaps
    vorticity = lambda line: inner[pl.ds(line, snaps, stride=lines), :]
    partial_gram[...] = gram_of(inside_lines(planes, lines // planes), vorticity, place, vort)


def outside_kernel(inner, left_w, right_w, place, partial_gram, vort, rows_out):
    snaps = vort.shape[1]
    planes = left_w.shape[1]
    lines = inner.shape[0] // snaps
    cols_x = lines // planes
    kept = place.shape[1]

    def vorticity(line):
        p, x = line // cols_x, line % cols_x
        value = inner[pl.ds(line, snaps, stride=lines), :]
        for h in range(REACH):
            if tap(cols_x + h - x):
                value = value + tap(cols_x + h - x) * right_w[h, p].astype(jnp.float32)
            if tap(h - REACH - x):
                value = value + tap(h - REACH - x) * left_w[h, p].astype(jnp.float32)
        return value

    gram = partial_gram[...] + gram_of(outside_lines(planes, cols_x), vorticity, place, vort)
    for part in range((snaps + kept) // kept):
        rows_out[:, 0, part * snaps : (part + 1) * snaps] = gram[part * kept : (part + 1) * kept]


def spread(tile, row):
    return jnp.broadcast_to(tile[row : row + 1], tile.shape)


def orthonormal_rows(block, inner):
    kept, snaps = block.shape
    shape = (GROUP, snaps)
    count = kept // GROUP
    row_at = index(shape, 0)
    inner = jnp.concatenate([inner, jnp.zeros((kept, snaps - kept), inner.dtype)], axis=1)
    inner_rows = [inner[GROUP * i : GROUP * (i + 1)] for i in range(count)]
    block_rows = [block[GROUP * i : GROUP * (i + 1)] for i in range(count)]
    for b in range(count):
        cols = []
        for t in range(GROUP):
            at = GROUP * b + t
            cols.append([jnp.broadcast_to(rows[:, at : at + 1], shape) for rows in inner_rows[b:]])
        pivot = [[spread(cols[t][0], i) for i in range(GROUP)] for t in range(GROUP)]
        cols = [col[1:] for col in cols]
        inner_at = [spread(inner_rows[b], t) for t in range(GROUP)]
        block_at = [spread(block_rows[b], t) for t in range(GROUP)]
        done = jnp.zeros(shape, jnp.float32)
        for t in range(GROUP):
            root = lax.rsqrt(pivot[t][t])
            inverse = root * root
            for later in range(t + 1, GROUP):
                part = pivot[t][later] * inverse
                for i in range(later, GROUP):
                    pivot[later][i] = pivot[later][i] - pivot[t][i] * part
                inner_at[later] = inner_at[later] - inner_at[t] * part
                block_at[later] = block_at[later] - block_at[t] * part
                cols[later] = [col - first * part for col, first in zip(cols[later], cols[t])]
            done = jnp.where(row_at == t, block_at[t] * root, done)
            inner_part = inner_at[t] * inverse
            block_part = block_at[t] * inverse
            for r in range(b + 1, count):
                inner_rows[r] = inner_rows[r] - cols[t][r - b - 1] * inner_part
                block_rows[r] = block_rows[r] - cols[t][r - b - 1] * block_part
        block_rows[b] = done
    return jnp.concatenate(block_rows, axis=0)


def modes_kernel(cells, rows, rank, start, vort_in, vort_out, modes, basis, work):
    kept, snaps = start.shape
    planes, cols_x = modes.shape[1:3]
    lines = planes * cols_x
    parts = [rows[:, 0, b * snaps : (b + 1) * snaps] for b in range(snaps // kept + 1)]
    gram = jnp.concatenate(parts[:-1], axis=0) * (1.0 / cells)
    picked = parts[-1]
    scale = jnp.where(rank[...] < kept, 1.0, 0.25).astype(jnp.float32)
    now = start[...]
    for step in range(ITERS):
        block = lax.dot_general(now * scale, gram, NT, precision=HIGHEST, preferred_element_type=jnp.float32)
        block = block * scale
        inner = lax.dot_general(block, block, NT, precision=HIGHEST, preferred_element_type=jnp.float32)
        now = orthonormal_rows(block, inner)
    coef = (now * scale).astype(jnp.bfloat16)
    anchor = jnp.sum(picked * coef.astype(jnp.float32), axis=1, keepdims=True)
    orient = anchor / jnp.maximum(jnp.abs(anchor), 1.0)
    basis[...] = now * orient
    for vort, held in (
        (vort_in, inside_lines(planes, cols_x)),
        (vort_out, outside_lines(planes, cols_x)),
    ):
        for at, line in enumerate(held):
            work[pl.ds(line, kept, stride=lines), :] = matmul(coef, vort[at]) * orient
    modes[...] = work[...].astype(jnp.bfloat16).reshape(modes.shape)


def local_place(anchor_index, planes, cols_x, cols_z, total_x, total_z):
    plane_of = anchor_index // (total_x * total_z)
    remain = anchor_index % (total_x * total_z)
    local_x = remain // total_z - lax.axis_index(GX) * cols_x
    local_z = remain % total_z - lax.axis_index(GZ) * cols_z
    owned = (local_x >= 0) & (local_x < cols_x) & (local_z >= 0) & (local_z < cols_z)
    return jnp.where(owned, (plane_of * cols_x + local_x) * cols_z + local_z, -1)


def size_of(axes):
    return math.prod(lax.axis_size(axis) for axis in ((axes,) if isinstance(axes, str) else axes))


def shifted(value, axis, step):
    count = size_of(axis)
    return lax.ppermute(value, axis, [(i, (i + step) % count) for i in range(count)])


def exchanged(rows, axis):
    return lax.all_to_all(rows, axis, 0, 0, tiled=True)


def total_kernel(share, rows, out):
    value = rows[:, 0, :]
    while value.shape[0] > share:
        count = value.shape[0] // share
        if count % 2 == 0:
            half = value.shape[0] // 2
            value = value[:half] + value[half:]
        else:
            value = sum(value[i * share : (i + 1) * share] for i in range(count))
    for at in range(0, out.shape[0], share):
        out[at : at + share, 0, :] = value


def totals(rows, share, axes):
    result = near((share * size_of(axes),) + rows.shape[1:], rows.dtype)
    return local_call(partial(total_kernel, share), [result], "total")(rows)[0]


def near(shape, dtype):
    return pltpu.VMEM(shape, dtype)


def local_call(kernel, outs, name, scratch=(), space=pltpu.VMEM):
    def run(*args):
        return pl.pallas_call(
            kernel,
            in_specs=[pl.BlockSpec(memory_space=space)] * len(args),
            out_specs=[pl.BlockSpec(memory_space=pltpu.VMEM)] * len(outs),
            out_shape=outs,
            scratch_shapes=list(scratch),
            compiler_params=pltpu.CompilerParams(vmem_limit_bytes=KERNEL_VMEM),
            name=name,
        )(*[pltpu.with_memory_space_constraint(arg, space) for arg in args])

    return run


def body(velocity, snapshot_rank, anchor_index, start_basis):
    _, snaps, planes, cols_x, cols_z = velocity.shape
    kept = start_basis.shape[1]
    lines = planes * cols_x
    total_x = cols_x * size_of(GX)
    total_z = cols_z * size_of(GZ)
    side = near((REACH, planes, snaps, cols_z), jnp.bfloat16)
    strip = near((GROUP, snaps * lines), jnp.bfloat16)
    rows_at = pltpu.VMEM((snaps * planes * GROUP, cols_z), jnp.float32)
    local = near((snaps, planes, cols_x, cols_z), jnp.bfloat16)
    head_w, tail_w, head_u, tail_u, wide, long = local_call(
        ends_kernel,
        [side, side, strip, strip, local, local],
        "ends",
        [rows_at, rows_at, pltpu.SemaphoreType.DMA((2 * LOADS,))],
        pltpu.HBM,
    )(velocity)
    left_w = shifted(tail_w, GX, 1)
    right_w = shifted(head_w, GX, -1)
    left_u = shifted(tail_u, GZ, 1)
    right_u = shifted(head_u, GZ, -1)
    field = near((snaps * lines, cols_z), jnp.float32)
    (inner,) = local_call(inner_kernel, [field], "inner")(long, wide)
    (inner,) = local_call(across_kernel, [field], "across")(inner, left_u, right_u)
    place = local_place(anchor_index, planes, cols_x, cols_z, total_x, total_z)
    within = len(inside_lines(planes, cols_x))
    vort_in, partial_gram = local_call(
        partial(inside_kernel, planes),
        [near((within, snaps, cols_z), jnp.bfloat16), near((snaps + kept, snaps), jnp.float32)],
        "inside",
    )(inner, place[None, :])
    vort_out, rows = local_call(
        outside_kernel,
        [
            near((lines - within, snaps, cols_z), jnp.bfloat16),
            near((kept, 1, (snaps // kept + 1) * snaps), jnp.float32),
        ],
        "outside",
    )(inner, left_w, right_w, place[None, :], partial_gram)
    part = kept // size_of(CHIPS)
    rows = totals(exchanged(rows, CHIPS), part, (CORES, GZ))
    rows = totals(exchanged(rows, (CORES, GZ)), part, CHIPS)
    rows = exchanged(rows, CHIPS)
    modes, basis = local_call(
        partial(modes_kernel, float(planes * total_x * total_z)),
        [
            jax.ShapeDtypeStruct((kept, planes, cols_x, cols_z), jnp.bfloat16),
            jax.ShapeDtypeStruct((kept, snaps), jnp.float32),
        ],
        "modes",
        [pltpu.VMEM((kept * lines, cols_z), jnp.float32)],
    )(rows, snapshot_rank[None, :], start_basis.T, vort_in, vort_out)
    return modes, basis.T


def solution(mesh):
    count_x, count_z = mesh.shape["gx"], mesh.shape["gz"]
    split = jax.sharding.Mesh(mesh.devices.reshape(count_x // 2, 2, count_z), (CHIPS, CORES, GZ))
    return jax.shard_map(
        body,
        mesh=split,
        in_specs=(P(None, None, None, GX, GZ), P(), P(), P()),
        out_specs=(P(None, None, GX, GZ), P()),
        check_vma=False,
    )
```

```python
import math
from functools import partial

import jax
import jax.numpy as jnp
from jax import lax
from jax.experimental import pallas as pl
from jax.experimental.pallas import tpu as pltpu
from jax.sharding import PartitionSpec as P

ITERS = 3
CHIPS = "chips"
CORES = "cores"
GX = (CHIPS, CORES)
GZ = "gz"
REACH = 3
TAPS = (45.0, -9.0, 1.0)
TAP_SUM = 60.0
GROUP = 8
FEW = 4
PIECES = 16
LOADS = 4
KERNEL_VMEM = 16 << 20
HIGHEST = lax.Precision.HIGHEST
NT = (((1,), (1,)), ((), ()))
TN = (((0,), (0,)), ((), ()))


def tap(offset):
    size = abs(offset)
    if size < 1 or size > REACH:
        return 0.0
    return TAPS[size - 1] if offset > 0 else -TAPS[size - 1]


def taps_at(offset):
    value = jnp.zeros(offset.shape, jnp.float32)
    for size in range(1, REACH + 1):
        value = jnp.where(offset == size, TAPS[size - 1], value)
        value = jnp.where(offset == -size, -TAPS[size - 1], value)
    return value


def index(shape, axis):
    return lax.broadcasted_iota(jnp.int32, shape, axis)


def twice(table):
    zero = jnp.zeros_like(table)
    return jnp.concatenate(
        [jnp.concatenate([table, zero], axis=1), jnp.concatenate([zero, table], axis=1)], axis=0
    ).astype(jnp.bfloat16)


def along_x_table(blocks, cols_x):
    shape = (blocks * cols_x, blocks * cols_x)
    row, col = index(shape, 0), index(shape, 1)
    inside = lax.div(row, cols_x) == lax.div(col, cols_x)
    return jnp.where(inside, taps_at(col - row), 0.0).astype(jnp.bfloat16)


def along_z_table(cols_z):
    shape = (cols_z, cols_z)
    return twice(-taps_at(index(shape, 0) - index(shape, 1)))


def edge_z_table(cols_z):
    shape = (2 * GROUP, cols_z)
    row, col = index(shape, 0), index(shape, 1)
    ahead = jnp.where(row < REACH, taps_at(cols_z + row - col), 0.0)
    behind = jnp.where((row >= GROUP) & (row < GROUP + REACH), taps_at(row - GROUP - REACH - col), 0.0)
    return twice(-(ahead + behind))


def ends_z_table(cols_z):
    shape = (2 * GROUP, cols_z)
    row, col = index(shape, 0), index(shape, 1)
    ahead = (row < REACH) & (col == row)
    behind = (row >= GROUP) & (row < GROUP + REACH) & (col == cols_z - REACH + row - GROUP)
    return jnp.where(ahead | behind, 1.0, 0.0).astype(jnp.bfloat16)


def matmul(left, right, dims=None):
    dims = dims or (((1,), (0,)), ((), ()))
    return lax.dot_general(left, right, dims, preferred_element_type=jnp.float32)


def flat_rows(field, start, count):
    block = field[start : start + count]
    return block.reshape(-1, block.shape[-1])


def two_blocks(field, start):
    return jnp.concatenate([flat_rows(field, start + at, FEW) for at in (0, FEW)], axis=1)


def ends_kernel(velocity, head_w, tail_w, head_u, tail_u, wide, long, first_rows, last_rows, landed):
    reach, planes, snaps, cols_z = head_w.shape
    cols_x = wide.shape[2]
    share = snaps // LOADS
    loads = []
    for field, near_field in ((1, wide), (0, long)):
        for part in range(LOADS):
            here = pl.ds(part * share, share)
            source = velocity.at[field, here]
            loads.append(pltpu.make_async_copy(source, near_field.at[here], landed.at[len(loads)]))
            loads[-1].start()
    stride = planes * GROUP
    for part in range(LOADS):
        loads[part].wait()
        here = slice(part * share, (part + 1) * share)
        rows = slice(part * share * stride, (part + 1) * share * stride)
        size = (share * stride, cols_z)
        first_rows[rows, :] = wide[here, :, :GROUP].reshape(size).astype(jnp.float32)
        last_rows[rows, :] = wide[here, :, cols_x - GROUP :].reshape(size).astype(jnp.float32)
        for p in range(planes):
            for h in range(reach):
                at = part * share * stride + p * GROUP + h
                head_w[h, p, here, :] = first_rows[pl.ds(at, share, stride=stride), :].astype(jnp.bfloat16)
                at = at + GROUP - reach
                tail_w[h, p, here, :] = last_rows[pl.ds(at, share, stride=stride), :].astype(jnp.bfloat16)
    ends_z = ends_z_table(cols_z)
    few = 2 * GROUP
    for part in range(LOADS):
        loads[LOADS + part].wait()
        for start in range(part * share, (part + 1) * share, few):
            span = slice(start * planes * cols_x, (start + few) * planes * cols_x)
            cols = matmul(ends_z, flat_rows(long, start, few), NT).astype(jnp.bfloat16)
            head_u[:, span] = cols[:GROUP]
            tail_u[:, span] = cols[GROUP:]


def inner_kernel(long, wide, out):
    planes, cols_x, cols_z = wide.shape[1:]
    count = FEW * planes * cols_x
    along_x = along_x_table(FEW * planes, cols_x)
    along_z = along_z_table(cols_z)
    for q in range(wide.shape[0] // (2 * FEW)):
        value = matmul(along_x, two_blocks(wide, 2 * FEW * q))
        value = value + matmul(two_blocks(long, 2 * FEW * q), along_z)
        for half in range(2):
            at = (2 * q + half) * count
            out[at : at + count, :] = value[:, half * cols_z : (half + 1) * cols_z]


def across_kernel(inner, left_u, right_u, out):
    cols_z = inner.shape[1]
    count = inner.shape[0] // PIECES
    edge_z = edge_z_table(cols_z)
    for q in range(PIECES // 2):
        spans = [slice((2 * q + half) * count, (2 * q + half + 1) * count) for half in range(2)]
        cols = jnp.concatenate([side[:, span] for span in spans for side in (right_u, left_u)], axis=0)
        value = matmul(cols, edge_z, TN)
        for half in range(2):
            out[spans[half], :] = inner[spans[half], :] + value[:, half * cols_z : (half + 1) * cols_z]


def inside_lines(planes, cols_x):
    return [p * cols_x + x for p in range(planes) for x in range(REACH, cols_x - REACH)]


def outside_lines(planes, cols_x):
    inside = set(inside_lines(planes, cols_x))
    return [line for line in range(planes * cols_x) if line not in inside]


def gram_of(lines, vorticity, place, vort):
    _, snaps, cols_z = vort.shape
    kept = place.shape[1]
    gram = jnp.zeros((snaps + kept, snaps), jnp.float32)
    lane = index((kept, 2 * cols_z), 1)
    down = jnp.broadcast_to(place[...].astype(jnp.float32), (GROUP, kept)).T[:, :1]
    for at in range(0, len(lines), 2):
        both = []
        for line in lines[at : at + 2]:
            value = (vorticity(line) * (1.0 / TAP_SUM)).astype(jnp.bfloat16)
            vort[at + len(both)] = value
            both.append(value)
        both = jnp.concatenate(both, axis=1)
        cell = lane + jnp.where(lane < cols_z, lines[at] * cols_z, (lines[at + 1] - 1) * cols_z)
        chosen = jnp.where(cell.astype(jnp.float32) == down, 1.0, 0.0).astype(jnp.bfloat16)
        gram = gram + matmul(jnp.concatenate([both, chosen], axis=0), both, NT)
    return gram


def inside_kernel(planes, inner, place, vort, partial_gram):
    snaps = vort.shape[1]
    lines = inner.shape[0] // snaps
    vorticity = lambda line: inner[pl.ds(line, snaps, stride=lines), :]
    partial_gram[...] = gram_of(inside_lines(planes, lines // planes), vorticity, place, vort)


def outside_kernel(inner, left_w, right_w, place, partial_gram, vort, rows_out):
    snaps = vort.shape[1]
    planes = left_w.shape[1]
    lines = inner.shape[0] // snaps
    cols_x = lines // planes
    kept = place.shape[1]

    def vorticity(line):
        p, x = line // cols_x, line % cols_x
        value = inner[pl.ds(line, snaps, stride=lines), :]
        for h in range(REACH):
            if tap(cols_x + h - x):
                value = value + tap(cols_x + h - x) * right_w[h, p].astype(jnp.float32)
            if tap(h - REACH - x):
                value = value + tap(h - REACH - x) * left_w[h, p].astype(jnp.float32)
        return value

    gram = partial_gram[...] + gram_of(outside_lines(planes, cols_x), vorticity, place, vort)
    for part in range((snaps + kept) // kept):
        rows_out[:, 0, part * snaps : (part + 1) * snaps] = gram[part * kept : (part + 1) * kept]


def spread(tile, row):
    return jnp.broadcast_to(tile[row : row + 1], tile.shape)


def orthonormal_rows(block, inner):
    kept, snaps = block.shape
    shape = (GROUP, snaps)
    count = kept // GROUP
    row_at = index(shape, 0)
    inner = jnp.concatenate([inner, jnp.zeros((kept, snaps - kept), inner.dtype)], axis=1)
    inner_rows = [inner[GROUP * i : GROUP * (i + 1)] for i in range(count)]
    block_rows = [block[GROUP * i : GROUP * (i + 1)] for i in range(count)]
    for b in range(count):
        cols = []
        for t in range(GROUP):
            at = GROUP * b + t
            cols.append([jnp.broadcast_to(rows[:, at : at + 1], shape) for rows in inner_rows[b:]])
        pivot = [[spread(cols[t][0], i) for i in range(GROUP)] for t in range(GROUP)]
        cols = [col[1:] for col in cols]
        inner_at = [spread(inner_rows[b], t) for t in range(GROUP)]
        block_at = [spread(block_rows[b], t) for t in range(GROUP)]
        done = jnp.zeros(shape, jnp.float32)
        for t in range(GROUP):
            root = lax.rsqrt(pivot[t][t])
            inverse = root * root
            for later in range(t + 1, GROUP):
                part = pivot[t][later] * inverse
                for i in range(later, GROUP):
                    pivot[later][i] = pivot[later][i] - pivot[t][i] * part
                inner_at[later] = inner_at[later] - inner_at[t] * part
                block_at[later] = block_at[later] - block_at[t] * part
                cols[later] = [col - first * part for col, first in zip(cols[later], cols[t])]
            done = jnp.where(row_at == t, block_at[t] * root, done)
            inner_part = inner_at[t] * inverse
            block_part = block_at[t] * inverse
            for r in range(b + 1, count):
                inner_rows[r] = inner_rows[r] - cols[t][r - b - 1] * inner_part
                block_rows[r] = block_rows[r] - cols[t][r - b - 1] * block_part
        block_rows[b] = done
    return jnp.concatenate(block_rows, axis=0)


def modes_kernel(cells, rows, rank, start, vort_in, vort_out, modes, basis, work):
    kept, snaps = start.shape
    planes, cols_x = modes.shape[1:3]
    lines = planes * cols_x
    parts = [rows[:, 0, b * snaps : (b + 1) * snaps] for b in range(snaps // kept + 1)]
    gram = jnp.concatenate(parts[:-1], axis=0) * (1.0 / cells)
    picked = parts[-1]
    scale = jnp.where(rank[...] < kept, 1.0, 0.25).astype(jnp.float32)
    now = start[...]
    for step in range(ITERS):
        block = lax.dot_general(now * scale, gram, NT, precision=HIGHEST, preferred_element_type=jnp.float32)
        block = block * scale
        inner = lax.dot_general(block, block, NT, precision=HIGHEST, preferred_element_type=jnp.float32)
        now = orthonormal_rows(block, inner)
    coef = (now * scale).astype(jnp.bfloat16)
    anchor = jnp.sum(picked * coef.astype(jnp.float32), axis=1, keepdims=True)
    orient = anchor / jnp.maximum(jnp.abs(anchor), 1.0)
    basis[...] = now * orient
    for vort, held in (
        (vort_in, inside_lines(planes, cols_x)),
        (vort_out, outside_lines(planes, cols_x)),
    ):
        for at, line in enumerate(held):
            work[pl.ds(line, kept, stride=lines), :] = matmul(coef, vort[at]) * orient
    modes[...] = work[...].astype(jnp.bfloat16).reshape(modes.shape)


def local_place(anchor_index, planes, cols_x, cols_z, total_x, total_z):
    plane_of = anchor_index // (total_x * total_z)
    remain = anchor_index % (total_x * total_z)
    local_x = remain // total_z - lax.axis_index(GX) * cols_x
    local_z = remain % total_z - lax.axis_index(GZ) * cols_z
    owned = (local_x >= 0) & (local_x < cols_x) & (local_z >= 0) & (local_z < cols_z)
    return jnp.where(owned, (plane_of * cols_x + local_x) * cols_z + local_z, -1)


def size_of(axes):
    return math.prod(lax.axis_size(axis) for axis in ((axes,) if isinstance(axes, str) else axes))


def shifted(value, axis, step):
    count = size_of(axis)
    return lax.ppermute(value, axis, [(i, (i + step) % count) for i in range(count)])


def exchanged(rows, axis):
    return lax.all_to_all(rows, axis, 0, 0, tiled=True)


def total_kernel(share, rows, out):
    value = rows[:, 0, :]
    while value.shape[0] > share:
        count = value.shape[0] // share
        if count % 2 == 0:
            half = value.shape[0] // 2
            value = value[:half] + value[half:]
        else:
            value = sum(value[i * share : (i + 1) * share] for i in range(count))
    for at in range(0, out.shape[0], share):
        out[at : at + share, 0, :] = value


def totals(rows, share, axes):
    result = near((share * size_of(axes),) + rows.shape[1:], rows.dtype)
    return local_call(partial(total_kernel, share), [result], "total")(rows)[0]


def near(shape, dtype):
    return pltpu.VMEM(shape, dtype)


def local_call(kernel, outs, name, scratch=(), space=pltpu.VMEM):
    def run(*args):
        return pl.pallas_call(
            kernel,
            in_specs=[pl.BlockSpec(memory_space=space)] * len(args),
            out_specs=[pl.BlockSpec(memory_space=pltpu.VMEM)] * len(outs),
            out_shape=outs,
            scratch_shapes=list(scratch),
            compiler_params=pltpu.CompilerParams(vmem_limit_bytes=KERNEL_VMEM),
            name=name,
        )(*[pltpu.with_memory_space_constraint(arg, space) for arg in args])

    return run


def body(velocity, snapshot_rank, anchor_index, start_basis):
    _, snaps, planes, cols_x, cols_z = velocity.shape
    kept = start_basis.shape[1]
    lines = planes * cols_x
    total_x = cols_x * size_of(GX)
    total_z = cols_z * size_of(GZ)
    side = near((REACH, planes, snaps, cols_z), jnp.bfloat16)
    strip = near((GROUP, snaps * lines), jnp.bfloat16)
    rows_at = pltpu.VMEM((snaps * planes * GROUP, cols_z), jnp.float32)
    local = near((snaps, planes, cols_x, cols_z), jnp.bfloat16)
    head_w, tail_w, head_u, tail_u, wide, long = local_call(
        ends_kernel,
        [side, side, strip, strip, local, local],
        "ends",
        [rows_at, rows_at, pltpu.SemaphoreType.DMA((2 * LOADS,))],
        pltpu.HBM,
    )(velocity)
    left_w = shifted(tail_w, GX, 1)
    right_w = shifted(head_w, GX, -1)
    left_u = shifted(tail_u, GZ, 1)
    right_u = shifted(head_u, GZ, -1)
    field = near((snaps * lines, cols_z), jnp.float32)
    (inner,) = local_call(inner_kernel, [field], "inner")(long, wide)
    (inner,) = local_call(across_kernel, [field], "across")(inner, left_u, right_u)
    place = local_place(anchor_index, planes, cols_x, cols_z, total_x, total_z)
    within = len(inside_lines(planes, cols_x))
    vort_in, partial_gram = local_call(
        partial(inside_kernel, planes),
        [near((within, snaps, cols_z), jnp.bfloat16), near((snaps + kept, snaps), jnp.float32)],
        "inside",
    )(inner, place[None, :])
    vort_out, rows = local_call(
        outside_kernel,
        [
            near((lines - within, snaps, cols_z), jnp.bfloat16),
            near((kept, 1, (snaps // kept + 1) * snaps), jnp.float32),
        ],
        "outside",
    )(inner, left_w, right_w, place[None, :], partial_gram)
    part = kept // size_of(CHIPS)
    rows = totals(exchanged(rows, CHIPS), part, (CORES, GZ))
    rows = totals(exchanged(rows, (CORES, GZ)), part, CHIPS)
    rows = exchanged(rows, CHIPS)
    modes, basis = local_call(
        partial(modes_kernel, float(planes * total_x * total_z)),
        [
            jax.ShapeDtypeStruct((kept, planes, cols_x, cols_z), jnp.bfloat16),
            jax.ShapeDtypeStruct((kept, snaps), jnp.float32),
        ],
        "modes",
        [pltpu.VMEM((kept * lines, cols_z), jnp.float32)],
    )(rows, snapshot_rank[None, :], start_basis.T, vort_in, vort_out)
    return modes, basis.T


def solution(mesh):
    count_x, count_z = mesh.shape["gx"], mesh.shape["gz"]
    split = jax.sharding.Mesh(mesh.devices.reshape(count_x // 2, 2, count_z), (CHIPS, CORES, GZ))
    return jax.shard_map(
        body,
        mesh=split,
        in_specs=(P(None, None, None, GX, GZ), P(), P(), P()),
        out_specs=(P(None, None, GX, GZ), P()),
        check_vma=False,
    )
```
